512 devices in a mesh: req: 32 (over y, x), exp: 16 (over z, core).
Axes of the slice: x: 4, y: 8, z: 8, core: 2. Of those that a mesh axis runs over, the one named last changes fastest.
Arguments:
- resid_in: bfloat16 [4096, 3584], P(('req', 'exp')), may hold values from -6 to 6
- queries: bfloat16 [4096, 3584], P(('req', 'exp')), may hold values from -40 to 40
- fresh_kv: bfloat16 [4096, 1024], P(('req', 'exp')), may hold values from -6 to 6
- kv_pool: bfloat16 [32, 16, 32, 16, 1024], P('req', 'exp'), may hold values from -6 to 6
- block_table: int32 [2048, 8], P(('req', 'exp')), may hold values from 0 to 31, as said below
- lengths: int32 [2048], P(('req', 'exp')), may hold values from 1 to 128, as said below
- mig_source: int32 [32, 16, 2, 4], P('req', 'exp'), may hold values from 0 to 31, as said below
- mig_target: int32 [32, 16, 2, 4], P('req', 'exp'), may hold values from 0 to 31, as said below
- expert_ids: int32 [4096, 8], P('req'), may hold values from 0 to 63, all different within a row; in each aligned block of 128 rows (0 to 127, 128 to 255, ...) at most 24 rows name the same one
- gate_values: float32 [4096, 8], P('req'), may hold values from 0.2 to 1
- norm_gain: bfloat16 [3584], replicated, may hold values from 0.5 to 1.5
- w_in: bfloat16 [16, 32, 3584, 256], P('exp', 'req'), may hold values from -0.09375 to 0.09375
- w_out: bfloat16 [16, 32, 256, 3584], P('exp', 'req'), may hold values from -0.125 to 0.125
Outputs:
- mixed: bfloat16 [4096, 3584], P(('req', 'exp'))
The draws below stay inside these ranges and needn't reach their ends.
Inputs may be any that keep to these rules, and one draw needn't show every extreme that they name: `block_table`: the entries of the 4 rows of one device are distinct pages of that device's pool. `lengths`: A request that arrives by migration has more than (3) * 16 cached positions. `mig_target`: on every device exactly one request arrives from req index - 1 and one from index + 1 (around the loop); [r, e, 0, i] is the page that takes page i of the request from index - 1, [r, e, 1, i] of the one from index + 1; they are the first 4 entries of that request's block-table row. `mig_source`: [r, e, 0, i] is the pool page sent as page i to index + 1, [r, e, 1, i] to index - 1; the 8 pages of a device are distinct and belong to no request that stays on it. `expert_ids`: each row names 8 different experts; among the 128 tokens of one index of req no expert is named by more than 24 rows.
All inputs are finite; a program needn't handle non-finite values.
Results may differ from the reference program's by a relative error of at most 0.012.
Values may be sent and summed in bfloat16 or wider, within the bound.
A program may use at most 64 MiB of HBM per device.

```python
import math
import jax
import jax.numpy as jnp
import numpy as np
from jax import lax

D = 3584
HEADS = 28
KV_HEADS = 4
HEAD_DIM = 128
TOPK = 8
EXPERTS = 64
FF = 2048
GRP = 8
FH = 256
REQ_DEV = 4
DRAFT = 2
TOK = 8
PAGE = 16
MAXP = 8
MIGP = 4
CTX = 128
KVW = 1024
PAGES_DEV = 32
REQUESTS = 2048
TOKENS = 4096
CAP = 24
N_REQ = 32
N_EXP = 16


def page_plan(key):
    base = jax.random.fold_in(key, 71)
    device_count = N_REQ * N_EXP
    order_key, slot_key, stay_key, move_key, rank_key = jax.random.split(base, 5)
    page_order = jax.vmap(lambda sub_key: jax.random.permutation(sub_key, PAGES_DEV))(jax.random.split(order_key, device_count))
    slot_order = jax.vmap(lambda sub_key: jax.random.permutation(sub_key, REQ_DEV))(jax.random.split(slot_key, device_count))
    tables = page_order.reshape(device_count, REQ_DEV, MAXP).astype(jnp.int32)
    from_left = slot_order[:, 0]
    from_right = slot_order[:, 1]
    first_stay = slot_order[:, 2]
    slot_ids = jnp.arange(REQ_DEV)[None, :]
    arriving = (slot_ids == from_left[:, None]) | (slot_ids == from_right[:, None])
    stay_lengths = jax.random.randint(stay_key, (device_count, REQ_DEV), 1, CTX + 1)
    move_lengths = jax.random.randint(move_key, (device_count, REQ_DEV), (MIGP - 1) * PAGE + 1, MIGP * PAGE + 1)
    request_lengths = jnp.where(arriving, move_lengths, stay_lengths)
    device_ids = jnp.arange(device_count)[:, None]
    request_lengths = jnp.where((device_ids == 0) & (slot_ids == first_stay[:, None]), CTX, request_lengths)
    request_lengths = jnp.where((device_ids == 0) & (slot_ids == from_left[:, None]), MIGP * PAGE, request_lengths).astype(jnp.int32)
    left_rows = jnp.take_along_axis(tables, from_left[:, None, None], axis=1)[:, 0, :MIGP]
    right_rows = jnp.take_along_axis(tables, from_right[:, None, None], axis=1)[:, 0, :MIGP]
    targets = jnp.stack([left_rows, right_rows], axis=1).astype(jnp.int32)
    page_counts = (request_lengths + PAGE - 1) // PAGE
    entry_used = jnp.logical_not(arriving)[:, :, None] & (jnp.arange(MAXP)[None, None, :] < page_counts[:, :, None])
    staying = jnp.any((tables[:, :, :, None] == jnp.arange(PAGES_DEV)[None, None, None, :]) & entry_used[:, :, :, None], axis=(1, 2))
    ranks = jax.vmap(lambda sub_key: jax.random.permutation(sub_key, PAGES_DEV))(jax.random.split(rank_key, device_count))
    ranks = (ranks + jnp.where(staying, PAGES_DEV, 0)).astype(jnp.int32)
    chosen = lax.top_k(-ranks, 2 * MIGP)[1].astype(jnp.int32)
    sources = jnp.stack([chosen[:, :MIGP], chosen[:, MIGP:]], axis=1)
    return (tables.reshape(REQUESTS, MAXP), request_lengths.reshape(REQUESTS), sources.reshape(N_REQ, N_EXP, 2, MIGP), targets.reshape(N_REQ, N_EXP, 2, MIGP))


def draw_block_table(key, part):
    return page_plan(key)[0]


def draw_lengths(key, part):
    return page_plan(key)[1]


def draw_mig_source(key, part):
    return page_plan(key)[2]


def draw_mig_target(key, part):
    return page_plan(key)[3]


def token_draws(key):
    base = jax.random.fold_in(key, 29)
    query_key, fresh_key = jax.random.split(base, 2)
    query_rows = jnp.clip(jax.random.normal(query_key, (TOKENS, HEADS * HEAD_DIM), jnp.float32), -6.0, 6.0)
    fresh_rows = jnp.clip(jax.random.normal(fresh_key, (TOKENS, KVW), jnp.float32), -6.0, 6.0)
    return (query_rows.astype(jnp.bfloat16), fresh_rows.astype(jnp.bfloat16))


def draw_queries(key, part):
    return token_draws(key)[0]


def draw_fresh_kv(key, part):
    return token_draws(key)[1]


def block_scale(key, shape, shards, smallest, high):
    level = 1.0
    for dim, parts in shards:
        draws = jax.random.uniform(jax.random.fold_in(jax.random.fold_in(key, 6), dim), (parts,), jnp.float32, smallest / len(shards), high / len(shards))
        level = level * jnp.repeat(jnp.exp(draws), shape[dim] // parts).reshape((-1,) + (1,) * (len(shape) - 1 - dim))
    return level


def routed_block(rng, own, number, rows, count, top, bound, skew):
    order = jax.random.permutation(rng, count)
    crowded, usual = portions_of(count, rows * top, bound, skew, True), portions_of(count, rows * top, bound, skew, False)
    places = jnp.arange(count)

    def named(sizes, turn):
        used = int((sizes > 0).sum())
        fixed = max(1, used // 4)
        passed = fixed + (places - fixed + turn * (used - fixed)) % max(1, count - fixed)
        return jnp.zeros((count,), jnp.int32).at[order[jnp.where(places < fixed, places, passed)]].set(jnp.asarray(sizes, jnp.int32))

    sizes = jnp.where(number % 4 == 0, named(crowded, number // 4), named(usual, number - number // 4 - 1))
    mixed = jax.random.permutation(jax.random.fold_in(own, 3), count)
    donor, receiver = mixed[0:count // 2 * 2:2], mixed[1:count // 2 * 2:2]
    margin = jnp.minimum(sizes[donor] - 1, bound - sizes[receiver]) // 2
    margin = jnp.where((donor == order[0]) | (receiver == order[0]) | (sizes[receiver] == 0), 0, jnp.maximum(margin, 0))
    passed = jax.random.randint(jax.random.fold_in(own, 4), (count // 2,), 0, 1 << 20) % (margin + 1)
    sizes = sizes.at[donor].add(-passed).at[receiver].add(passed)
    labels = jnp.searchsorted(jnp.cumsum(sizes), jnp.arange(rows * top), side="right").astype(jnp.int32)
    table = labels.reshape(top, rows).T
    table = table[jax.random.permutation(jax.random.fold_in(own, 1), rows)]
    turn = jax.random.randint(jax.random.fold_in(own, 2), (rows, 1), 0, top)
    return jnp.take_along_axis(table, (jnp.arange(top)[None, :] + turn) % top, axis=1)


def portions_of(number_of, total, reach, slope, full):
    loads = [(1 << 20) // math.isqrt(standing ** slope) + 1 for standing in range(1, number_of + 1)]
    largest = reach if full else min(reach, max(-(-total // number_of), total * loads[0] // sum(loads)))
    least = 1 if total - largest >= number_of - 1 else 0
    holding, spare = [largest] + [least] * (number_of - 1), total - largest - least * (number_of - 1)
    while spare > 0:
        candidates = [i for i in range(1, number_of) if holding[i] < largest] or [i for i in range(1, number_of) if holding[i] < reach]
        mass, left = sum([loads[i] for i in candidates]), spare
        for i in candidates:
            addition = min(reach - holding[i], max(1, left * loads[i] // mass), spare)
            holding[i] = holding[i] + addition
            spare = spare - addition
    return np.array(holding)


def bell_draw(stream_key, dims, deviation, bound, shards=(), kind=jnp.bfloat16):
    result = deviation * jax.random.normal(stream_key, dims, jnp.float32)
    if shards:
        result = result * block_scale(stream_key, dims, shards, -0.22, 0.18)
    return jnp.clip(result, -bound, bound).astype(kind)


def setup_inputs(seed: int = 0) -> dict:
    splits = jax.random.split(jax.random.key(seed), 14)
    resid_in = bell_draw(splits[0], (TOKENS, D), 1.0, 6.0, ((0, 512),))
    queries = draw_queries(jax.random.fold_in(splits[13], 71), 0)
    fresh_kv = draw_fresh_kv(jax.random.fold_in(splits[13], 71), 0)
    kv_pool = bell_draw(splits[3], (N_REQ, N_EXP, PAGES_DEV, PAGE, KVW), 1.0, 6.0, ((0, 32), (1, 16)))
    block_table = draw_block_table(jax.random.fold_in(splits[13], 71), 0)
    lengths = draw_lengths(jax.random.fold_in(splits[13], 71), 0)
    mig_source = draw_mig_source(jax.random.fold_in(splits[13], 71), 0)
    mig_target = draw_mig_target(jax.random.fold_in(splits[13], 71), 0)
    expert_ids_keys = jax.random.split(jax.random.fold_in(splits[8], 1), TOKENS // (N_EXP * TOK))
    expert_ids_turns = jax.random.permutation(jax.random.fold_in(splits[8], 3), TOKENS // (N_EXP * TOK))
    expert_ids = jax.vmap(lambda own, number: routed_block(jax.random.fold_in(splits[8], 2), own, number, N_EXP * TOK, EXPERTS, TOPK, CAP, 1))(expert_ids_keys, expert_ids_turns).reshape((TOKENS, TOPK))
    gate_values = jnp.clip(0.2 + 0.8 * jax.random.uniform(splits[9], (TOKENS, TOPK), jnp.float32) ** block_scale(splits[9], (TOKENS, TOPK), ((0, 32),), -0.2, 0.2), 0.2, 1.0)
    norm_gain = jnp.clip(1.0 + 0.1 * jax.random.normal(splits[10], (D,), jnp.float32), 0.5, 1.5).astype(jnp.bfloat16)
    w_in = bell_draw(splits[11], (N_EXP, N_REQ, D, FH), D ** -0.5, 0.09375, ((0, 16), (1, 32)))
    w_out = bell_draw(splits[12], (N_EXP, N_REQ, FH, D), FF ** -0.5, 0.125, ((0, 16), (1, 32)))
    return dict(resid_in=resid_in, queries=queries, fresh_kv=fresh_kv, kv_pool=kv_pool, block_table=block_table, lengths=lengths, mig_source=mig_source, mig_target=mig_target, expert_ids=expert_ids, gate_values=gate_values, norm_gain=norm_gain, w_in=w_in, w_out=w_out)


neg_big = -1e+30
norm_eps = 1e-06

def pick_pages(pool_pages, page_ids):
    return jax.vmap(jax.vmap(lambda device_pages, device_ids: device_pages[device_ids]))(pool_pages, page_ids)

def migrate(kv_pool, mig_source, mig_target):
    to_next = pick_pages(kv_pool, mig_source[:, :, 0])
    to_prev = pick_pages(kv_pool, mig_source[:, :, 1])
    arrived = jnp.concatenate([jnp.roll(to_next, 1, axis=0), jnp.roll(to_prev, -1, axis=0)], axis=2)
    targets = jnp.concatenate([mig_target[:, :, 0], mig_target[:, :, 1]], axis=2)
    return jax.vmap(jax.vmap(lambda device_pages, device_ids, incoming: device_pages.at[device_ids].set(incoming)))(kv_pool, targets, arrived)

def attend_device(packed):
    pages, table, request_lengths, query_rows, fresh_rows = packed
    group_size = HEADS // KV_HEADS
    key_width = KV_HEADS * HEAD_DIM
    span = CTX + DRAFT
    cache = pages[table].reshape(REQ_DEV, CTX, KVW)
    stacked = jnp.concatenate([cache, fresh_rows.reshape(REQ_DEV, DRAFT, KVW)], axis=1).astype(jnp.float32)
    key_part = stacked[:, :, :key_width].reshape(REQ_DEV, span, KV_HEADS, HEAD_DIM)
    value_part = stacked[:, :, key_width:].reshape(REQ_DEV, span, KV_HEADS, HEAD_DIM)
    query_part = query_rows.astype(jnp.float32).reshape(REQ_DEV, DRAFT, KV_HEADS, group_size, HEAD_DIM)
    scores = jnp.einsum('rdkgh,rpkh->rdkgp', query_part, key_part, precision=lax.Precision.HIGHEST) * HEAD_DIM ** (-0.5)
    position = jnp.arange(span)
    draft_index = jnp.arange(DRAFT)
    in_cache = position[None, None, :] < request_lengths[:, None, None]
    in_draft = (position[None, :] >= CTX) & (position[None, :] - CTX <= draft_index[:, None])
    visible = jnp.where(position[None, None, :] < CTX, in_cache, in_draft[None, :, :])
    live = visible[:, :, None, None, :]
    scores = jnp.where(live, scores, neg_big)
    highest = lax.optimization_barrier(jnp.max(scores, axis=-1, keepdims=True))
    weights = jnp.where(live, jnp.exp(scores - highest), 0.0)
    weight_sum = lax.optimization_barrier(jnp.sum(weights, axis=-1))
    summed = jnp.einsum('rdkgp,rpkh->rdkgh', weights, value_part, precision=lax.Precision.HIGHEST)
    return (summed / weight_sum[..., None]).reshape(TOK, HEADS * HEAD_DIM)

def reference(resid_in, queries, fresh_kv, kv_pool, block_table, lengths, mig_source, mig_target, expert_ids, gate_values, norm_gain, w_in, w_out):
    device_count = N_REQ * N_EXP
    pool_after = migrate(kv_pool, mig_source, mig_target)
    attention = lax.map(attend_device, (pool_after.reshape(device_count, PAGES_DEV, PAGE, KVW), block_table.reshape(device_count, REQ_DEV, MAXP), lengths.reshape(device_count, REQ_DEV), queries.reshape(device_count, TOK, D), fresh_kv.reshape(device_count, TOK, KVW)))
    residual = resid_in.astype(jnp.float32) + attention.reshape(TOKENS, D)
    inv_rms = lax.rsqrt(lax.optimization_barrier(jnp.mean(residual * residual, axis=1, keepdims=True)) + norm_eps)
    normed = (residual * inv_rms * norm_gain.astype(jnp.float32)).astype(jnp.bfloat16)
    inner_all = w_in.reshape(EXPERTS, GRP, D, FH)
    outer_all = w_out.reshape(EXPERTS, GRP, FH, D)
    limit_rows = N_REQ * CAP

    def one_expert(running, packed):
        inner_weights, outer_weights, expert = packed
        matches = expert_ids == expert
        named_rows = jnp.any(matches, axis=1)
        gate_weight = lax.optimization_barrier(jnp.sum(jnp.where(matches, gate_values, 0.0), axis=1))
        row_index = jnp.nonzero(named_rows, size=limit_rows, fill_value=0)[0].astype(jnp.int32)
        is_valid = jnp.arange(limit_rows) < jnp.sum(named_rows.astype(jnp.int32))
        inputs = normed[row_index].astype(jnp.float32)
        hidden = jnp.einsum('td,sdf->stf', inputs, inner_weights.astype(jnp.float32), precision=lax.Precision.HIGHEST)
        activated = lax.optimization_barrier(jax.nn.silu(hidden).astype(jnp.bfloat16)).astype(jnp.float32)
        partials = jnp.einsum('stf,sfd->std', activated, outer_weights.astype(jnp.float32), precision=lax.Precision.HIGHEST)
        partials = lax.optimization_barrier(partials.astype(jnp.bfloat16)).astype(jnp.float32)
        combined = lax.optimization_barrier(jnp.sum(partials, axis=0)) * jnp.where(is_valid, gate_weight[row_index], 0.0)[:, None]
        return (running.at[row_index].add(combined), None)
    expert_mix, unused = lax.scan(one_expert, jnp.zeros((TOKENS, D), jnp.float32), (inner_all, outer_all, jnp.arange(EXPERTS, dtype=jnp.int32)))
    return (residual + expert_mix).astype(jnp.bfloat16)
```

```python
import functools

import jax
import jax.numpy as jnp
from jax import lax
from jax.experimental import pallas as pl
from jax.experimental.pallas import tpu as pltpu
from jax.sharding import PartitionSpec as P

HEADS = 28
KV_HEADS = 4
HEAD_DIM = 128
EXP_DEV = 4
CAP = 24
NX = 4
NY = 8
CHUNKS = 7

neg_big = -1e30
norm_eps = 1e-06
MESH = pl.DeviceIdType.MESH


def with_halo(block, sides, width):
    for axis, dim in sides:
        count = lax.axis_size(axis)
        forward = [(i, i + 1) for i in range(count - 1)]
        forward.append((count - 1, 0))
        backward = [(target, source) for source, target in forward]
        low = lax.ppermute(
            lax.slice_in_dim(block, block.shape[dim] - width, None, axis=dim), axis, forward
        )
        high = lax.ppermute(lax.slice_in_dim(block, 0, width, axis=dim), axis, backward)
        block = jnp.concatenate([low, block, high], axis=dim)
    return block


def partial_attention(query_grid, key_rows, visible):
    request_count = key_rows.shape[0]
    span = key_rows.shape[1]
    key_width = KV_HEADS * HEAD_DIM
    key_part = key_rows[:, :, :key_width].reshape(request_count, span, KV_HEADS, HEAD_DIM)
    value_part = (
        key_rows[:, :, key_width:]
        .reshape(request_count, span, KV_HEADS, HEAD_DIM)
        .astype(jnp.float32)
    )
    scores = jnp.einsum(
        "rdkgh,rpkh->rdkgp", query_grid, key_part, preferred_element_type=jnp.float32
    ) * HEAD_DIM ** (-0.5)
    live = visible[:, :, None, None, :]
    scores = jnp.where(live, scores, neg_big)
    highest = jnp.max(scores, axis=-1)
    weights = jnp.where(live, jnp.exp(scores - highest[..., None]), 0.0)
    weight_sum = jnp.sum(weights, axis=-1)
    summed = jnp.einsum("rdkgp,rpkh->rdkgh", weights, value_part, precision=lax.Precision.HIGHEST)
    return (highest, weight_sum, summed)


def wait_bytes(ref, sem):
    pltpu.make_async_copy(ref, ref, sem).wait()


def moe_kernel(
    packed,
    mix_hi,
    mix_lo,
    w_in,
    w_out,
    out,
    grid_in,
    part,
    relay_in,
    direct_in,
    summed,
    back,
    w1,
    w2,
    hidden,
    act,
    load_sem,
    own_sem,
    y_send,
    y_recv,
    x_send,
    x_recv,
    r_send,
    r_recv,
    br_send,
    br_recv,
    bd_send,
    bd_recv,
    by_own,
    by_send,
    by_recv,
):
    me = lax.axis_index("req")
    ex = lax.axis_index("exp")
    x = lax.rem(me, NX)
    y = lax.div(me, NX)
    width = w1.shape[0] // CHUNKS
    row = y * NX
    xp = lax.rem(x + 1, NX)
    xm = lax.rem(x + NX - 1, NX)
    xo = lax.rem(x + 2, NX)
    right = (row + xp, ex)
    left = (row + xm, ex)

    def ydev(j):
        yd = lax.rem(y + j, NY)
        return yd, (yd * NX + x, ex)

    barrier = pltpu.get_barrier_semaphore()
    for peer in (left, right):
        pl.semaphore_signal(barrier, inc=1, device_id=peer, device_id_type=MESH)
    for j in range(1, NY):
        pl.semaphore_signal(barrier, inc=1, device_id=ydev(j)[1], device_id_type=MESH)
    load1 = pltpu.make_async_copy(w_in, w1, load_sem.at[0])
    load2 = pltpu.make_async_copy(w_out, w2, load_sem.at[1])
    load1.start()
    load2.start()
    hidden[...] = jnp.zeros_like(hidden)
    pl.semaphore_wait(barrier, 2 + NY - 1)

    def span(i):
        return pl.ds(pl.multiple_of(i * width, 128), width)

    def remote(src, dst, send, recv, dev):
        return pltpu.make_async_remote_copy(
            src_ref=src, dst_ref=dst, send_sem=send, recv_sem=recv, device_id=dev, device_id_type=MESH
        )

    def issue_y(i, c):
        cols = span(i)
        pltpu.make_async_copy(
            packed.at[lax.div(y, 2), :, cols], grid_in.at[x, y, :, cols], own_sem.at[i]
        ).start()
        for j in range(1, NY):
            yd, dev = ydev(j)
            remote(
                packed.at[lax.div(yd, 2), :, cols],
                grid_in.at[x, y, :, cols],
                y_send.at[i],
                y_recv.at[i],
                dev,
            ).start()
        return c

    lax.fori_loop(0, CHUNKS, issue_y, 0)
    load1.wait()
    low, high = pl.ds(0, NY // 2), pl.ds(NY // 2, NY // 2)

    def seven(i):
        return grid_in.at[0, pl.ds(0, NY - 1), :, span(i)]

    def inward(i, c):
        @pl.when(i < CHUNKS)
        def _():
            cols = span(i)
            wait_bytes(grid_in.at[0, 0, :, cols], own_sem.at[i])
            wait_bytes(seven(i), y_recv.at[i])
            block = grid_in.at[x, :, :, cols]
            remote(block, block, x_send.at[i, 0], x_recv.at[i, 0], right).start()
            remote(block, block, x_send.at[i, 1], x_recv.at[i, 1], left).start()

        @pl.when((i >= 1) & (i < CHUNKS + 1))
        def _():
            n = i - 1
            cols = span(n)
            wait_bytes(grid_in.at[xm, :, :, cols], x_recv.at[n, 0])
            block = grid_in.at[xm, low, :, cols]
            remote(block, block, r_send.at[n, 0], r_recv.at[n, 0], right).start()
            wait_bytes(grid_in.at[xp, :, :, cols], x_recv.at[n, 1])
            block = grid_in.at[xp, high, :, cols]
            remote(block, block, r_send.at[n, 1], r_recv.at[n, 1], left).start()

        @pl.when(i >= 2)
        def _():
            n = i - 2
            cols = span(n)
            wait_bytes(grid_in.at[xo, low, :, cols], r_recv.at[n, 0])
            wait_bytes(grid_in.at[xo, high, :, cols], r_recv.at[n, 1])
            weight = w1[span(n), :]
            for b in range(NX):
                hidden[b] += jnp.dot(
                    grid_in[b, :, :, cols].reshape(NY * CAP, width),
                    weight,
                    preferred_element_type=jnp.float32,
                )

        return c

    lax.fori_loop(0, CHUNKS + 2, inward, 0)
    for b in range(NX):
        v = hidden[b]
        act[b] = (v / (1.0 + jnp.exp(-v))).astype(jnp.bfloat16)
    load2.wait()

    def outward(i, c):
        @pl.when(i < CHUNKS)
        def _():
            cols = span(i)

            def product(b):
                part[b, :, :, cols] = (
                    jnp.dot(act[b], w2[:, cols], preferred_element_type=jnp.float32)
                    .astype(jnp.bfloat16)
                    .reshape(NY, CAP, width)
                )

            product(xo)
            product(xm)
            product(xp)
            remote(
                part.at[xo, low, :, cols], relay_in.at[0, :, :, cols],
                br_send.at[i, 0], br_recv.at[i, 0], left,
            ).start()
            remote(
                part.at[xo, high, :, cols], relay_in.at[1, :, :, cols],
                br_send.at[i, 1], br_recv.at[i, 1], right,
            ).start()
            product(x)
            remote(
                part.at[xm, high, :, cols], direct_in.at[0, high, :, cols],
                bd_send.at[i, 0], bd_recv.at[i, 0], left,
            ).start()
            remote(
                part.at[xp, low, :, cols], direct_in.at[1, low, :, cols],
                bd_send.at[i, 1], bd_recv.at[i, 1], right,
            ).start()

        @pl.when((i >= 1) & (i < CHUNKS + 1))
        def _():
            n = i - 1
            cols = span(n)

            def added(b, rows, side):
                wait_bytes(relay_in.at[side, :, :, cols], br_recv.at[n, side])
                part[b, rows, :, cols] = (
                    part[b, rows, :, cols].astype(jnp.float32)
                    + relay_in[side, :, :, cols].astype(jnp.float32)
                ).astype(jnp.bfloat16)

            added(xm, low, 0)
            added(xp, high, 1)
            remote(
                part.at[xm, low, :, cols], direct_in.at[0, low, :, cols],
                bd_send.at[n, 2], bd_recv.at[n, 2], left,
            ).start()
            remote(
                part.at[xp, high, :, cols], direct_in.at[1, high, :, cols],
                bd_send.at[n, 3], bd_recv.at[n, 3], right,
            ).start()

        @pl.when((i >= 2) & (i < CHUNKS + 2))
        def _():
            n = i - 2
            cols = span(n)
            wait_bytes(direct_in.at[0, high, :, cols], bd_recv.at[n, 0])
            wait_bytes(direct_in.at[1, low, :, cols], bd_recv.at[n, 1])
            wait_bytes(direct_in.at[0, low, :, cols], bd_recv.at[n, 2])
            wait_bytes(direct_in.at[1, high, :, cols], bd_recv.at[n, 3])
            summed[:, :, cols] = (
                part[x, :, :, cols].astype(jnp.float32)
                + direct_in[0, :, :, cols].astype(jnp.float32)
                + direct_in[1, :, :, cols].astype(jnp.float32)
            ).astype(jnp.bfloat16)
            pltpu.make_async_copy(
                summed.at[y, :, cols], back.at[y, :, cols], by_own.at[n]
            ).start()
            for j in range(1, NY):
                yd, dev = ydev(j)
                remote(
                    summed.at[yd, :, cols], back.at[y, :, cols], by_send.at[n], by_recv.at[n], dev
                ).start()

        @pl.when(i >= 3)
        def _():
            n = i - 3
            cols = span(n)
            wait_bytes(back.at[0, :, cols], by_own.at[n])
            wait_bytes(back.at[pl.ds(0, NY - 1), :, cols], by_recv.at[n])
            rows = back[:, :, cols].reshape(NY * CAP, width)
            out[:, cols] = (
                jnp.dot(mix_hi[...], rows, preferred_element_type=jnp.float32)
                + jnp.dot(mix_lo[...], rows, preferred_element_type=jnp.float32)
            ).astype(jnp.bfloat16)

        return c

    lax.fori_loop(0, CHUNKS + 3, outward, 0)

    def drain(i, c):
        cols = span(i)
        half = relay_in.at[0, :, :, cols]
        wait_bytes(seven(i), y_send.at[i])
        for s in range(2):
            wait_bytes(grid_in.at[0, :, :, cols], x_send.at[i, s])
            wait_bytes(half, r_send.at[i, s])
            wait_bytes(half, br_send.at[i, s])
        for s in range(4):
            wait_bytes(half, bd_send.at[i, s])
        wait_bytes(back.at[pl.ds(0, NY - 1), :, cols], by_send.at[i])
        return c

    lax.fori_loop(0, CHUNKS, drain, 0)


def moe(packed, mix_hi, mix_lo, w_in, w_out):
    depth, units = w_in.shape
    bf = jnp.bfloat16
    vmem = pl.BlockSpec(memory_space=pltpu.VMEM)
    anywhere = pl.BlockSpec(memory_space=pl.ANY)
    dma = pltpu.SemaphoreType.DMA
    return pl.pallas_call(
        moe_kernel,
        name="moe_plane",
        out_shape=jax.ShapeDtypeStruct((mix_hi.shape[0], depth), bf),
        in_specs=[vmem, vmem, vmem, anywhere, anywhere],
        out_specs=vmem,
        scratch_shapes=[
            pltpu.VMEM((NX, NY, CAP, depth), bf),
            pltpu.VMEM((NX, NY, CAP, depth), bf),
            pltpu.VMEM((2, NY // 2, CAP, depth), bf),
            pltpu.VMEM((2, NY, CAP, depth), bf),
            pltpu.VMEM((NY, CAP, depth), bf),
            pltpu.VMEM((NY, CAP, depth), bf),
            pltpu.VMEM((depth, units), bf),
            pltpu.VMEM((units, depth), bf),
            pltpu.VMEM((NX, NY * CAP, units), jnp.float32),
            pltpu.VMEM((NX, NY * CAP, units), bf),
            dma((2,)),
            dma((CHUNKS,)),
            dma((CHUNKS,)),
            dma((CHUNKS,)),
            dma((CHUNKS, 2)),
            dma((CHUNKS, 2)),
            dma((CHUNKS, 2)),
            dma((CHUNKS, 2)),
            dma((CHUNKS, 2)),
            dma((CHUNKS, 2)),
            dma((CHUNKS, 4)),
            dma((CHUNKS, 4)),
            dma((CHUNKS,)),
            dma((CHUNKS,)),
            dma((CHUNKS,)),
        ],
        compiler_params=pltpu.CompilerParams(
            collective_id=0, has_side_effects=True, vmem_limit_bytes=56 * 1024 * 1024
        ),
    )(packed, mix_hi, mix_lo, w_in, w_out)


def body(
    resid_in,
    queries,
    fresh_kv,
    kv_pool,
    block_table,
    lengths,
    mig_source,
    mig_target,
    expert_ids,
    gate_values,
    norm_gain,
    w_in,
    w_out,
):
    request_count = block_table.shape[0]
    table_width = block_table.shape[1]
    page_tokens = kv_pool.shape[3]
    kv_width = kv_pool.shape[4]
    cache_span = table_width * page_tokens
    token_count = resid_in.shape[0]
    draft_count = token_count // request_count
    model_width = resid_in.shape[1]
    moved = mig_source.shape[3]
    pool_pages = kv_pool[0, 0]
    sources = mig_source[0, 0]
    target_pairs = mig_target[0, 0]
    outgoing = jnp.concatenate([pool_pages[sources[1]], pool_pages[sources[0]]], axis=0)
    targets = jnp.concatenate([target_pairs[0], target_pairs[1]], axis=0)
    extended = with_halo(outgoing, (("req", 0),), moved)
    arrivals = jnp.concatenate([extended[:moved], extended[-moved:]], axis=0)
    query_grid = queries.reshape(request_count, draft_count, KV_HEADS, HEADS // KV_HEADS, HEAD_DIM)
    fresh_rows = fresh_kv.reshape(request_count, draft_count, kv_width)
    position = jnp.arange(cache_span)
    cache_visible = jnp.broadcast_to(
        position[None, None, :] < lengths[:, None, None], (request_count, draft_count, cache_span)
    )
    draft_index = jnp.arange(draft_count)
    draft_visible = jnp.broadcast_to(
        draft_index[None, :] <= draft_index[:, None], (request_count, draft_count, draft_count)
    )
    pool_after = pool_pages.at[targets].set(arrivals)
    cache_rows = pool_after[block_table].reshape(request_count, cache_span, kv_width)
    parts = partial_attention(
        query_grid,
        jnp.concatenate([cache_rows, fresh_rows], axis=1),
        jnp.concatenate([cache_visible, draft_visible], axis=2),
    )
    attention = (parts[2] / parts[1][..., None]).reshape(token_count, model_width)
    residual = resid_in.astype(jnp.float32) + attention
    inv_rms = lax.rsqrt(jnp.mean(residual * residual, axis=1, keepdims=True) + norm_eps)
    normed = (residual * inv_rms * norm_gain.astype(jnp.float32)).astype(jnp.bfloat16)
    local_ids = lax.axis_index("exp") * EXP_DEV + jnp.arange(EXP_DEV)
    matches = expert_ids[None, :, :] == local_ids[:, None, None]
    is_named = jnp.any(matches, axis=2)
    gate_local = jnp.sum(jnp.where(matches, gate_values[None, :, :], 0.0), axis=2)
    slot_index = jnp.cumsum(is_named.astype(jnp.int32), axis=1) - 1
    placement = is_named[:, None, :] & (slot_index[:, None, :] == jnp.arange(CAP)[None, :, None])
    slot_select = placement.astype(jnp.bfloat16)
    packed = jnp.einsum(
        "kct,td->kcd",
        slot_select,
        lax.all_gather(normed, "exp", axis=0, tiled=True),
        preferred_element_type=jnp.float32,
    ).astype(jnp.bfloat16)
    gated = jnp.where(placement, gate_local[:, None, :], 0.0)
    gated = jnp.broadcast_to(gated[:, None], (EXP_DEV, NY // EXP_DEV) + gated.shape[1:])
    mix = gated.reshape(NY * CAP, -1).T
    mix_hi = lax.reduce_precision(mix, 8, 7)
    mix_lo = (mix - mix_hi).astype(jnp.bfloat16)
    mixed_rows = moe(packed, mix_hi.astype(jnp.bfloat16), mix_lo, w_in[0, 0], w_out[0, 0])
    expert_mix = lax.psum_scatter(mixed_rows, "exp", scatter_dimension=0, tiled=True).astype(
        jnp.float32
    )
    return (residual + expert_mix).astype(jnp.bfloat16)


def solution(mesh):
    placed = (
        P(("req", "exp"), None),
        P(("req", "exp"), None),
        P(("req", "exp"), None),
        P("req", "exp", None, None, None),
        P(("req", "exp"), None),
        P(("req", "exp")),
        P("req", "exp", None, None),
        P("req", "exp", None, None),
        P("req", None),
        P("req", None),
        P(),
        P("exp", "req", None, None),
        P("exp", "req", None, None),
    )
    return jax.shard_map(
        body, mesh=mesh, in_specs=placed, out_specs=P(("req", "exp"), None), check_vma=False
    )
```

```python
import functools

import jax
import jax.numpy as jnp
from jax import lax
from jax.experimental import pallas as pl
from jax.experimental.pallas import tpu as pltpu
from jax.sharding import PartitionSpec as P

HEADS = 28
KV_HEADS = 4
HEAD_DIM = 128
EXP_DEV = 4
CAP = 24
NX = 4
NY = 8
NZ = 8
CHUNKS = 7

neg_big = -1e30
norm_eps = 1e-06
MESH = pl.DeviceIdType.MESH


def with_halo(block, sides, width):
    for axis, dim in sides:
        count = lax.axis_size(axis)
        forward = [(i, i + 1) for i in range(count - 1)]
        forward.append((count - 1, 0))
        backward = [(target, source) for source, target in forward]
        low = lax.ppermute(
            lax.slice_in_dim(block, block.shape[dim] - width, None, axis=dim), axis, forward
        )
        high = lax.ppermute(lax.slice_in_dim(block, 0, width, axis=dim), axis, backward)
        block = jnp.concatenate([low, block, high], axis=dim)
    return block


def partial_attention(query_grid, key_rows, visible):
    request_count = key_rows.shape[0]
    span = key_rows.shape[1]
    key_width = KV_HEADS * HEAD_DIM
    key_part = key_rows[:, :, :key_width].reshape(request_count, span, KV_HEADS, HEAD_DIM)
    value_part = (
        key_rows[:, :, key_width:]
        .reshape(request_count, span, KV_HEADS, HEAD_DIM)
        .astype(jnp.float32)
    )
    scores = jnp.einsum(
        "rdkgh,rpkh->rdkgp", query_grid, key_part, preferred_element_type=jnp.float32
    ) * HEAD_DIM ** (-0.5)
    live = visible[:, :, None, None, :]
    scores = jnp.where(live, scores, neg_big)
    highest = jnp.max(scores, axis=-1)
    weights = jnp.where(live, jnp.exp(scores - highest[..., None]), 0.0)
    weight_sum = jnp.sum(weights, axis=-1)
    summed = jnp.einsum("rdkgp,rpkh->rdkgh", weights, value_part, precision=lax.Precision.HIGHEST)
    return (highest, weight_sum, summed)


def wait_bytes(ref, sem):
    pltpu.make_async_copy(ref, ref, sem).wait()


def moe_kernel(
    normed,
    select,
    mix_hi,
    mix_lo,
    residual,
    w_in,
    w_out,
    out,
    tokens,
    packed,
    mixed,
    mixed_send,
    core_in,
    z_out,
    z_in,
    grid_in,
    part,
    relay_in,
    direct_in,
    summed,
    back,
    w1,
    w2,
    hidden,
    act,
    load_sem,
    own_sem,
    y_send,
    y_recv,
    x_send,
    x_recv,
    r_send,
    r_recv,
    br_send,
    br_recv,
    bd_send,
    bd_recv,
    by_own,
    by_send,
    by_recv,
    z_own,
    z_send,
    z_recv,
    c_send,
    c_recv,
    bc_send,
    bc_recv,
    bz_own,
    bz_send,
    bz_recv,
):
    me = lax.axis_index("req")
    ex = lax.axis_index("exp")
    x = lax.rem(me, NX)
    y = lax.div(me, NX)
    width = w1.shape[0] // CHUNKS
    row = y * NX
    xp = lax.rem(x + 1, NX)
    xm = lax.rem(x + NX - 1, NX)
    xo = lax.rem(x + 2, NX)
    right = (row + xp, ex)
    left = (row + xm, ex)

    def ydev(j):
        yd = lax.rem(y + j, NY)
        return yd, (yd * NX + x, ex)

    z = lax.div(ex, 2)
    core = lax.rem(ex, 2)
    other = 1 - core
    partner = (me, z * 2 + other)

    def zdev(j):
        zd = lax.rem(z + j, NZ)
        return zd, (me, zd * 2 + core)

    barrier = pltpu.get_barrier_semaphore()
    for j in range(1, NZ):
        pl.semaphore_signal(barrier, inc=1, device_id=zdev(j)[1], device_id_type=MESH)
    for peer in (partner, left, right):
        pl.semaphore_signal(barrier, inc=1, device_id=peer, device_id_type=MESH)
    for j in range(1, NY):
        pl.semaphore_signal(barrier, inc=1, device_id=ydev(j)[1], device_id_type=MESH)
    load1 = pltpu.make_async_copy(w_in, w1, load_sem.at[0])
    load2 = pltpu.make_async_copy(w_out, w2, load_sem.at[1])
    load1.start()
    load2.start()
    hidden[...] = jnp.zeros_like(hidden)
    pl.semaphore_wait(barrier, 3 + NY - 1 + NZ - 1)

    def span(i):
        return pl.ds(pl.multiple_of(i * width, 128), width)

    def remote(src, dst, send, recv, dev):
        return pltpu.make_async_remote_copy(
            src_ref=src, dst_ref=dst, send_sem=send, recv_sem=recv, device_id=dev, device_id_type=MESH
        )

    def issue_z(i, c):
        cols = span(i)
        mine = tokens.at[z, core, :, cols]
        pltpu.make_async_copy(normed.at[:, cols], mine, z_own.at[i]).start()
        for j in range(1, NZ):
            remote(normed.at[:, cols], mine, z_send.at[i], z_recv.at[i], zdev(j)[1]).start()
        return c

    lax.fori_loop(0, CHUNKS, issue_z, 0)
    load1.wait()
    low, high = pl.ds(0, NY // 2), pl.ds(NY // 2, NY // 2)

    def seven(i):
        return grid_in.at[0, pl.ds(0, NY - 1), :, span(i)]

    def inward(i, c):
        @pl.when(i < CHUNKS)
        def _():
            cols = span(i)
            wait_bytes(tokens.at[0, 0, :, cols], z_own.at[i])
            wait_bytes(tokens.at[pl.ds(0, NZ - 1), 0, :, cols], z_recv.at[i])
            block = tokens.at[:, core, :, cols]
            remote(block, block, c_send.at[i], c_recv.at[i], partner).start()

        @pl.when((i >= 1) & (i < CHUNKS + 1))
        def _():
            n = i - 1
            cols = span(n)
            wait_bytes(tokens.at[:, 0, :, cols], c_recv.at[n])
            packed[:, :, cols] = (
                jnp.dot(
                    select[...],
                    tokens[:, :, :, cols].reshape(select.shape[1], width),
                    preferred_element_type=jnp.float32,
                )
                .astype(jnp.bfloat16)
                .reshape(EXP_DEV, CAP, width)
            )
            pltpu.make_async_copy(
                packed.at[lax.div(y, 2), :, cols], grid_in.at[x, y, :, cols], own_sem.at[n]
            ).start()
            for j in range(1, NY):
                yd, dev = ydev(j)
                remote(
                    packed.at[lax.div(yd, 2), :, cols],
                    grid_in.at[x, y, :, cols],
                    y_send.at[n],
                    y_recv.at[n],
                    dev,
                ).start()

        @pl.when((i >= 2) & (i < CHUNKS + 2))
        def _():
            n = i - 2
            cols = span(n)
            wait_bytes(grid_in.at[0, 0, :, cols], own_sem.at[n])
            wait_bytes(seven(n), y_recv.at[n])
            block = grid_in.at[x, :, :, cols]
            remote(block, block, x_send.at[n, 0], x_recv.at[n, 0], right).start()
            remote(block, block, x_send.at[n, 1], x_recv.at[n, 1], left).start()

        @pl.when((i >= 3) & (i < CHUNKS + 3))
        def _():
            n = i - 3
            cols = span(n)
            wait_bytes(grid_in.at[xm, :, :, cols], x_recv.at[n, 0])
            block = grid_in.at[xm, low, :, cols]
            remote(block, block, r_send.at[n, 0], r_recv.at[n, 0], right).start()
            wait_bytes(grid_in.at[xp, :, :, cols], x_recv.at[n, 1])
            block = grid_in.at[xp, high, :, cols]
            remote(block, block, r_send.at[n, 1], r_recv.at[n, 1], left).start()

        @pl.when(i >= 4)
        def _():
            n = i - 4
            cols = span(n)
            wait_bytes(grid_in.at[xo, low, :, cols], r_recv.at[n, 0])
            wait_bytes(grid_in.at[xo, high, :, cols], r_recv.at[n, 1])
            weight = w1[span(n), :]
            for b in range(NX):
                hidden[b] += jnp.dot(
                    grid_in[b, :, :, cols].reshape(NY * CAP, width),
                    weight,
                    preferred_element_type=jnp.float32,
                )

        return c

    lax.fori_loop(0, CHUNKS + 4, inward, 0)
    for b in range(NX):
        v = hidden[b]
        act[b] = (v / (1.0 + jnp.exp(-v))).astype(jnp.bfloat16)
    load2.wait()

    def outward(i, c):
        @pl.when(i < CHUNKS)
        def _():
            cols = span(i)

            def product(b):
                part[b, :, :, cols] = (
                    jnp.dot(act[b], w2[:, cols], preferred_element_type=jnp.float32)
                    .astype(jnp.bfloat16)
                    .reshape(NY, CAP, width)
                )

            product(xo)
            product(xm)
            product(xp)
            remote(
                part.at[xo, low, :, cols], relay_in.at[0, :, :, cols],
                br_send.at[i, 0], br_recv.at[i, 0], left,
            ).start()
            remote(
                part.at[xo, high, :, cols], relay_in.at[1, :, :, cols],
                br_send.at[i, 1], br_recv.at[i, 1], right,
            ).start()
            product(x)
            remote(
                part.at[xm, high, :, cols], direct_in.at[0, high, :, cols],
                bd_send.at[i, 0], bd_recv.at[i, 0], left,
            ).start()
            remote(
                part.at[xp, low, :, cols], direct_in.at[1, low, :, cols],
                bd_send.at[i, 1], bd_recv.at[i, 1], right,
            ).start()

        @pl.when((i >= 1) & (i < CHUNKS + 1))
        def _():
            n = i - 1
            cols = span(n)

            def added(b, rows, side):
                wait_bytes(relay_in.at[side, :, :, cols], br_recv.at[n, side])
                part[b, rows, :, cols] = (
                    part[b, rows, :, cols].astype(jnp.float32)
                    + relay_in[side, :, :, cols].astype(jnp.float32)
                ).astype(jnp.bfloat16)

            added(xm, low, 0)
            added(xp, high, 1)
            remote(
                part.at[xm, low, :, cols], direct_in.at[0, low, :, cols],
                bd_send.at[n, 2], bd_recv.at[n, 2], left,
            ).start()
            remote(
                part.at[xp, high, :, cols], direct_in.at[1, high, :, cols],
                bd_send.at[n, 3], bd_recv.at[n, 3], right,
            ).start()

        @pl.when((i >= 2) & (i < CHUNKS + 2))
        def _():
            n = i - 2
            cols = span(n)
            wait_bytes(direct_in.at[0, high, :, cols], bd_recv.at[n, 0])
            wait_bytes(direct_in.at[1, low, :, cols], bd_recv.at[n, 1])
            wait_bytes(direct_in.at[0, low, :, cols], bd_recv.at[n, 2])
            wait_bytes(direct_in.at[1, high, :, cols], bd_recv.at[n, 3])
            summed[:, :, cols] = (
                part[x, :, :, cols].astype(jnp.float32)
                + direct_in[0, :, :, cols].astype(jnp.float32)
                + direct_in[1, :, :, cols].astype(jnp.float32)
            ).astype(jnp.bfloat16)
            pltpu.make_async_copy(
                summed.at[y, :, cols], back.at[y, :, cols], by_own.at[n]
            ).start()
            for j in range(1, NY):
                yd, dev = ydev(j)
                remote(
                    summed.at[yd, :, cols], back.at[y, :, cols], by_send.at[n], by_recv.at[n], dev
                ).start()

        @pl.when((i >= 3) & (i < CHUNKS + 3))
        def _():
            n = i - 3
            cols = span(n)
            wait_bytes(back.at[0, :, cols], by_own.at[n])
            wait_bytes(back.at[pl.ds(0, NY - 1), :, cols], by_recv.at[n])
            rows = back[:, :, cols].reshape(NY * CAP, width)
            total = jnp.dot(mix_hi[...], rows, preferred_element_type=jnp.float32) + jnp.dot(
                mix_lo[...], rows, preferred_element_type=jnp.float32
            )
            total = total.reshape(NZ, 2, -1, width)
            mixed[:, :, :, cols] = total
            mixed_send[:, :, :, cols] = total.astype(jnp.bfloat16)
            remote(
                mixed_send.at[:, other, :, cols], core_in.at[:, :, cols],
                bc_send.at[n], bc_recv.at[n], partner,
            ).start()

        @pl.when((i >= 4) & (i < CHUNKS + 4))
        def _():
            n = i - 4
            cols = span(n)
            wait_bytes(core_in.at[:, :, cols], bc_recv.at[n])
            z_out[:, :, cols] = (
                mixed[:, core, :, cols] + core_in[:, :, cols].astype(jnp.float32)
            ).astype(jnp.bfloat16)
            pltpu.make_async_copy(z_out.at[z, :, cols], z_in.at[z, :, cols], bz_own.at[n]).start()
            for j in range(1, NZ):
                zd, dev = zdev(j)
                remote(
                    z_out.at[zd, :, cols], z_in.at[z, :, cols], bz_send.at[n], bz_recv.at[n], dev
                ).start()

        @pl.when(i >= 5)
        def _():
            n = i - 5
            cols = span(n)
            wait_bytes(z_in.at[0, :, cols], bz_own.at[n])
            wait_bytes(z_in.at[pl.ds(0, NZ - 1), :, cols], bz_recv.at[n])
            total = residual[:, cols]
            for k in range(NZ):
                total = total + z_in[k, :, cols].astype(jnp.float32)
            out[:, cols] = total.astype(jnp.bfloat16)

        return c

    lax.fori_loop(0, CHUNKS + 5, outward, 0)

    def drain(i, c):
        cols = span(i)
        half = relay_in.at[0, :, :, cols]
        wait_bytes(seven(i), y_send.at[i])
        for s in range(2):
            wait_bytes(grid_in.at[0, :, :, cols], x_send.at[i, s])
            wait_bytes(half, r_send.at[i, s])
            wait_bytes(half, br_send.at[i, s])
        for s in range(4):
            wait_bytes(half, bd_send.at[i, s])
        wait_bytes(back.at[pl.ds(0, NY - 1), :, cols], by_send.at[i])
        wait_bytes(z_in.at[pl.ds(0, NZ - 1), :, cols], z_send.at[i])
        wait_bytes(z_in.at[:, :, cols], c_send.at[i])
        wait_bytes(z_in.at[:, :, cols], bc_send.at[i])
        wait_bytes(z_in.at[pl.ds(0, NZ - 1), :, cols], bz_send.at[i])
        return c

    lax.fori_loop(0, CHUNKS, drain, 0)


def moe(normed, select, mix_hi, mix_lo, residual, w_in, w_out):
    depth, units = w_in.shape
    rows = normed.shape[0]
    bf = jnp.bfloat16
    vmem = pl.BlockSpec(memory_space=pltpu.VMEM)
    anywhere = pl.BlockSpec(memory_space=pl.ANY)
    dma = pltpu.SemaphoreType.DMA
    return pl.pallas_call(
        moe_kernel,
        name="moe_slice",
        out_shape=jax.ShapeDtypeStruct((rows, depth), bf),
        in_specs=[vmem, vmem, vmem, vmem, vmem, anywhere, anywhere],
        out_specs=vmem,
        scratch_shapes=[
            pltpu.VMEM((NZ, 2, rows, depth), bf),
            pltpu.VMEM((EXP_DEV, CAP, depth), bf),
            pltpu.VMEM((NZ, 2, rows, depth), jnp.float32),
            pltpu.VMEM((NZ, 2, rows, depth), bf),
            pltpu.VMEM((NZ, rows, depth), bf),
            pltpu.VMEM((NZ, rows, depth), bf),
            pltpu.VMEM((NZ, rows, depth), bf),
            pltpu.VMEM((NX, NY, CAP, depth), bf),
            pltpu.VMEM((NX, NY, CAP, depth), bf),
            pltpu.VMEM((2, NY // 2, CAP, depth), bf),
            pltpu.VMEM((2, NY, CAP, depth), bf),
            pltpu.VMEM((NY, CAP, depth), bf),
            pltpu.VMEM((NY, CAP, depth), bf),
            pltpu.VMEM((depth, units), bf),
            pltpu.VMEM((units, depth), bf),
            pltpu.VMEM((NX, NY * CAP, units), jnp.float32),
            pltpu.VMEM((NX, NY * CAP, units), bf),
            dma((2,)),
            dma((CHUNKS,)),
            dma((CHUNKS,)),
            dma((CHUNKS,)),
            dma((CHUNKS, 2)),
            dma((CHUNKS, 2)),
            dma((CHUNKS, 2)),
            dma((CHUNKS, 2)),
            dma((CHUNKS, 2)),
            dma((CHUNKS, 2)),
            dma((CHUNKS, 4)),
            dma((CHUNKS, 4)),
            dma((CHUNKS,)),
            dma((CHUNKS,)),
            dma((CHUNKS,)),
        ]
        + [dma((CHUNKS,))] * 10,
        compiler_params=pltpu.CompilerParams(
            collective_id=0, has_side_effects=True, vmem_limit_bytes=56 * 1024 * 1024
        ),
    )(normed, select, mix_hi, mix_lo, residual, w_in, w_out)


def body(
    resid_in,
    queries,
    fresh_kv,
    kv_pool,
    block_table,
    lengths,
    mig_source,
    mig_target,
    expert_ids,
    gate_values,
    norm_gain,
    w_in,
    w_out,
):
    request_count = block_table.shape[0]
    table_width = block_table.shape[1]
    page_tokens = kv_pool.shape[3]
    kv_width = kv_pool.shape[4]
    cache_span = table_width * page_tokens
    token_count = resid_in.shape[0]
    draft_count = token_count // request_count
    model_width = resid_in.shape[1]
    moved = mig_source.shape[3]
    pool_pages = kv_pool[0, 0]
    sources = mig_source[0, 0]
    target_pairs = mig_target[0, 0]
    outgoing = jnp.concatenate([pool_pages[sources[1]], pool_pages[sources[0]]], axis=0)
    targets = jnp.concatenate([target_pairs[0], target_pairs[1]], axis=0)
    extended = with_halo(outgoing, (("req", 0),), moved)
    arrivals = jnp.concatenate([extended[:moved], extended[-moved:]], axis=0)
    query_grid = queries.reshape(request_count, draft_count, KV_HEADS, HEADS // KV_HEADS, HEAD_DIM)
    fresh_rows = fresh_kv.reshape(request_count, draft_count, kv_width)
    position = jnp.arange(cache_span)
    cache_visible = jnp.broadcast_to(
        position[None, None, :] < lengths[:, None, None], (request_count, draft_count, cache_span)
    )
    draft_index = jnp.arange(draft_count)
    draft_visible = jnp.broadcast_to(
        draft_index[None, :] <= draft_index[:, None], (request_count, draft_count, draft_count)
    )
    pool_after = pool_pages.at[targets].set(arrivals)
    cache_rows = pool_after[block_table].reshape(request_count, cache_span, kv_width)
    parts = partial_attention(
        query_grid,
        jnp.concatenate([cache_rows, fresh_rows], axis=1),
        jnp.concatenate([cache_visible, draft_visible], axis=2),
    )
    attention = (parts[2] / parts[1][..., None]).reshape(token_count, model_width)
    residual = resid_in.astype(jnp.float32) + attention
    inv_rms = lax.rsqrt(jnp.mean(residual * residual, axis=1, keepdims=True) + norm_eps)
    normed = (residual * inv_rms * norm_gain.astype(jnp.float32)).astype(jnp.bfloat16)
    local_ids = lax.axis_index("exp") * EXP_DEV + jnp.arange(EXP_DEV)
    matches = expert_ids[None, :, :] == local_ids[:, None, None]
    is_named = jnp.any(matches, axis=2)
    gate_local = jnp.sum(jnp.where(matches, gate_values[None, :, :], 0.0), axis=2)
    slot_index = jnp.cumsum(is_named.astype(jnp.int32), axis=1) - 1
    placement = is_named[:, None, :] & (slot_index[:, None, :] == jnp.arange(CAP)[None, :, None])
    select = placement.astype(jnp.bfloat16).reshape(EXP_DEV * CAP, -1)
    gated = jnp.where(placement, gate_local[:, None, :], 0.0)
    gated = jnp.broadcast_to(gated[:, None], (EXP_DEV, NY // EXP_DEV) + gated.shape[1:])
    mix = gated.reshape(NY * CAP, -1).T
    mix_hi = lax.reduce_precision(mix, 8, 7)
    mix_lo = (mix - mix_hi).astype(jnp.bfloat16)
    return moe(
        normed, select, mix_hi.astype(jnp.bfloat16), mix_lo, residual, w_in[0, 0], w_out[0, 0]
    )


def solution(mesh):
    placed = (
        P(("req", "exp"), None),
        P(("req", "exp"), None),
        P(("req", "exp"), None),
        P("req", "exp", None, None, None),
        P(("req", "exp"), None),
        P(("req", "exp")),
        P("req", "exp", None, None),
        P("req", "exp", None, None),
        P("req", None),
        P("req", None),
        P(),
        P("exp", "req", None, None),
        P("exp", "req", None, None),
    )
    return jax.shard_map(
        body, mesh=mesh, in_specs=placed, out_specs=P(("req", "exp"), None), check_vma=False
    )
```

```python
import functools

import jax
import jax.numpy as jnp
from jax import lax
from jax.experimental import pallas as pl
from jax.experimental.pallas import tpu as pltpu
from jax.sharding import PartitionSpec as P

HEADS = 28
KV_HEADS = 4
HEAD_DIM = 128
EXP_DEV = 4
CAP = 24
TOK = 8
MIGP = 4
NX = 4
NY = 8
NZ = 8
CHUNKS = 14
LAG = 3

neg_big = -1e30
norm_eps = 1e-06
MESH = pl.DeviceIdType.MESH


def wait_bytes(ref, sem):
    pltpu.make_async_copy(ref, ref, sem).wait()


def choose_slots(ex, ids, gates, select, mix_hi, mix_lo):
    count = ids.shape[1]
    earlier = lax.broadcasted_iota(jnp.int32, (count, count), 0)
    later = lax.broadcasted_iota(jnp.int32, (count, count), 1)
    upto = jnp.where(earlier <= later, 1.0, 0.0).astype(jnp.bfloat16)
    slot = lax.broadcasted_iota(jnp.int32, (CAP, count), 0).astype(jnp.float32) + 1.0
    for k in range(EXP_DEV):
        match = ids[...] == ex * EXP_DEV + k
        named = jnp.max(jnp.where(match, 1.0, 0.0), axis=0, keepdims=True)
        gate = jnp.sum(jnp.where(match, gates[...], 0.0), axis=0, keepdims=True)
        row = jnp.broadcast_to(named, (8, count)).astype(jnp.bfloat16)
        order = jnp.dot(row, upto, preferred_element_type=jnp.float32)[:1]
        placed = jnp.where(slot == order, 1.0, 0.0) * named
        select[k] = placed.astype(jnp.bfloat16)
        weight = placed * gate
        upper = weight.astype(jnp.bfloat16)
        lower = (weight - upper.astype(jnp.float32)).astype(jnp.bfloat16)
        for h in range(NY // EXP_DEV):
            mix_hi[k * (NY // EXP_DEV) + h] = upper
            mix_lo[k * (NY // EXP_DEV) + h] = lower


def attend(table, lengths, targets, resid_in, queries, fresh, pool, gain, arriving, cache, residual, normed):
    requests, entries = table.shape
    page = pool.shape[1]
    context = entries * page
    drafts = TOK // requests
    group = HEADS // KV_HEADS

    def gather(i, c):
        entry = table[lax.div(i, entries), lax.rem(i, entries)]
        moved = jnp.int32(0)
        place = jnp.int32(0)
        for side in range(2):
            for p in range(MIGP):
                same = entry == targets[side, p]
                moved = jnp.where(same, 1, moved)
                place = jnp.where(same, side * MIGP + p, place)
        new = arriving[lax.div(place, MIGP), lax.rem(place, MIGP)].astype(jnp.float32)
        old = pool[entry].astype(jnp.float32)
        taken = jnp.broadcast_to(moved, new.shape) > 0
        cache[pl.ds(pl.multiple_of(i * page, page), page), :] = jnp.where(taken, new, old).astype(
            jnp.bfloat16
        )
        return c

    lax.fori_loop(0, requests * entries, gather, 0)
    shape = (group * TOK, requests * context)
    token = lax.rem(lax.broadcasted_iota(jnp.int32, shape, 0), TOK)
    column = lax.broadcasted_iota(jnp.int32, shape, 1)
    holder = lax.div(column, context)
    limit = jnp.zeros(shape, jnp.int32)
    for n in range(requests):
        limit = jnp.where(holder == n, lengths[n], limit)
    cached = (lax.div(token, drafts) == holder) & (lax.rem(column, context) < limit)
    shape = (group * TOK, TOK)
    token = lax.rem(lax.broadcasted_iota(jnp.int32, shape, 0), TOK)
    column = lax.broadcasted_iota(jnp.int32, shape, 1)
    drafted = (lax.div(token, drafts) == lax.div(column, drafts)) & (column <= token)
    values = KV_HEADS * HEAD_DIM
    contract = (((1,), (1,)), ((), ()))

    def weighted(weights, rows):
        upper = weights.astype(jnp.bfloat16)
        lower = (weights - upper.astype(jnp.float32)).astype(jnp.bfloat16)
        return jnp.dot(upper, rows, preferred_element_type=jnp.float32) + jnp.dot(
            lower, rows, preferred_element_type=jnp.float32
        )

    squares = jnp.zeros((TOK, 1), jnp.float32)
    for kv in range(KV_HEADS):
        key_cols = slice(kv * HEAD_DIM, (kv + 1) * HEAD_DIM)
        value_cols = slice(values + kv * HEAD_DIM, values + (kv + 1) * HEAD_DIM)
        heads = [slice(h * HEAD_DIM, (h + 1) * HEAD_DIM) for h in range(kv * group, (kv + 1) * group)]
        query = jnp.concatenate([queries[:, h].astype(jnp.float32) for h in heads], axis=0).astype(
            jnp.bfloat16
        )
        far = lax.dot_general(
            query, cache[:, key_cols], contract, preferred_element_type=jnp.float32
        ) * HEAD_DIM ** (-0.5)
        near = lax.dot_general(
            query, fresh[:, key_cols], contract, preferred_element_type=jnp.float32
        ) * HEAD_DIM ** (-0.5)
        far = jnp.where(cached, far, neg_big)
        near = jnp.where(drafted, near, neg_big)
        highest = jnp.maximum(
            jnp.max(far, axis=1, keepdims=True), jnp.max(near, axis=1, keepdims=True)
        )
        far = jnp.where(cached, jnp.exp(far - highest), 0.0)
        near = jnp.where(drafted, jnp.exp(near - highest), 0.0)
        total = jnp.sum(far, axis=1, keepdims=True) + jnp.sum(near, axis=1, keepdims=True)
        attention = (
            weighted(far, cache[:, value_cols]) + weighted(near, fresh[:, value_cols])
        ) / total
        for g, h in enumerate(heads):
            mine = resid_in[:, h].astype(jnp.float32) + attention[g * TOK : (g + 1) * TOK]
            residual[:, h] = mine
            squares = squares + jnp.sum(mine * mine, axis=1, keepdims=True)
    inverse = lax.rsqrt(squares / (HEADS * HEAD_DIM) + norm_eps)
    normed[...] = (residual[...] * inverse * gain[...].astype(jnp.float32)).astype(jnp.bfloat16)


def layer_kernel(
    table,
    lengths,
    sources,
    targets,
    resid_in,
    queries,
    fresh,
    pool,
    ids,
    gates,
    gain,
    w_in,
    w_out,
    out,
    leaving,
    arriving,
    cache,
    residual,
    normed,
    select,
    mix_hi,
    mix_lo,
    tokens,
    packed,
    mixed,
    mixed_send,
    core_in,
    z_out,
    z_in,
    grid_in,
    part,
    relay_in,
    direct_in,
    summed,
    back,
    w1,
    w2,
    hidden,
    act,
    load_sem,
    page_send,
    page_recv,
    own_sem,
    y_send,
    y_recv,
    x_send,
    x_recv,
    r_send,
    r_recv,
    br_send,
    br_recv,
    bd_send,
    bd_recv,
    by_own,
    by_send,
    by_recv,
    z_own,
    z_send,
    z_recv,
    c_send,
    c_recv,
    bc_send,
    bc_recv,
    bz_own,
    bz_send,
    bz_recv,
):
    me = lax.axis_index("req")
    ex = lax.axis_index("exp")
    x = lax.rem(me, NX)
    y = lax.div(me, NX)
    width = w1.shape[0] // CHUNKS
    row = y * NX
    xp = lax.rem(x + 1, NX)
    xm = lax.rem(x + NX - 1, NX)
    xo = lax.rem(x + 2, NX)
    ring = NX * NY
    after = (lax.rem(me + 1, ring), ex)
    before = (lax.rem(me + ring - 1, ring), ex)
    right = (row + xp, ex)
    left = (row + xm, ex)

    def ydev(j):
        yd = lax.rem(y + j, NY)
        return yd, (yd * NX + x, ex)

    z = lax.div(ex, 2)
    core = lax.rem(ex, 2)
    other = 1 - core
    partner = (me, z * 2 + other)

    def zdev(j):
        zd = lax.rem(z + j, NZ)
        return zd, (me, zd * 2 + core)

    barrier = pltpu.get_barrier_semaphore()
    for j in range(1, NZ):
        pl.semaphore_signal(barrier, inc=1, device_id=zdev(j)[1], device_id_type=MESH)
    for peer in (partner, left, right, after, before):
        pl.semaphore_signal(barrier, inc=1, device_id=peer, device_id_type=MESH)
    for j in range(1, NY):
        pl.semaphore_signal(barrier, inc=1, device_id=ydev(j)[1], device_id_type=MESH)
    load1 = pltpu.make_async_copy(w_in, w1, load_sem.at[0])
    load2 = pltpu.make_async_copy(w_out, w2, load_sem.at[1])
    load1.start()
    load2.start()
    for i in range(MIGP):
        leaving[0, i] = pool[sources[0, i]]
        leaving[1, i] = pool[sources[1, i]]
    hidden[...] = jnp.zeros_like(hidden)
    pl.semaphore_wait(barrier, 5 + NY - 1 + NZ - 1)

    def span(i):
        return pl.ds(pl.multiple_of(i * width, 128), width)

    def remote(src, dst, send, recv, dev):
        return pltpu.make_async_remote_copy(
            src_ref=src, dst_ref=dst, send_sem=send, recv_sem=recv, device_id=dev, device_id_type=MESH
        )

    pages = [
        remote(leaving.at[side], arriving.at[side], page_send.at[side], page_recv.at[side], dev)
        for side, dev in ((0, after), (1, before))
    ]
    for copy in pages:
        copy.start()
    choose_slots(ex, ids, gates, select, mix_hi, mix_lo)
    for copy in pages:
        copy.wait_recv()
    attend(table, lengths, targets, resid_in, queries, fresh, pool, gain, arriving, cache, residual, normed)

    def issue_z(i, c):
        cols = span(i)
        mine = tokens.at[i, z, core]
        pltpu.make_async_copy(normed.at[:, cols], mine, z_own.at[i]).start()
        for j in range(1, NZ):
            remote(normed.at[:, cols], mine, z_send.at[i], z_recv.at[i], zdev(j)[1]).start()
        return c

    lax.fori_loop(0, CHUNKS, issue_z, 0)
    load1.wait()
    low, high = pl.ds(0, NY // 2), pl.ds(NY // 2, NY // 2)

    def seven(i):
        return grid_in.at[i, 0, pl.ds(0, NY - 1)]

    def inward(i, c):
        @pl.when(i < CHUNKS)
        def _():
            cols = span(i)
            wait_bytes(tokens.at[i, 0, 0], z_own.at[i])
            wait_bytes(tokens.at[i, pl.ds(0, NZ - 1), 0], z_recv.at[i])
            block = tokens.at[i, :, core]
            remote(block, block, c_send.at[i], c_recv.at[i], partner).start()

        @pl.when((i >= 1 * LAG) & (i < CHUNKS + 1 * LAG))
        def _():
            n = i - 1 * LAG
            cols = span(n)
            wait_bytes(tokens.at[n, :, 0], c_recv.at[n])
            packed[n] = (
                jnp.dot(
                    select[...].reshape(EXP_DEV * CAP, NZ * 2 * TOK),
                    tokens[n].reshape(NZ * 2 * TOK, width),
                    preferred_element_type=jnp.float32,
                )
                .astype(jnp.bfloat16)
                .reshape(EXP_DEV, CAP, width)
            )
            mine = packed.at[n, lax.div(y, 2)]
            pltpu.make_async_copy(mine, grid_in.at[n, x, 0], own_sem.at[n]).start()
            remote(mine, grid_in.at[n, x, 0], x_send.at[n, 0], x_recv.at[n, 0], right).start()
            remote(mine, grid_in.at[n, x, 0], x_send.at[n, 1], x_recv.at[n, 1], left).start()
            for j in range(1, NY):
                yd, dev = ydev(j)
                remote(
                    packed.at[n, lax.div(yd, 2)],
                    grid_in.at[n, x, NY - j],
                    y_send.at[n],
                    y_recv.at[n],
                    dev,
                ).start()

        @pl.when((i >= 2 * LAG) & (i < CHUNKS + 2 * LAG))
        def _():
            n = i - 2 * LAG
            cols = span(n)
            wait_bytes(seven(n), y_recv.at[n])
            block = grid_in.at[n, x, pl.ds(1, NY - 1)]
            remote(block, block, x_send.at[n, 0], x_recv.at[n, 0], right).start()
            remote(block, block, x_send.at[n, 1], x_recv.at[n, 1], left).start()

        @pl.when((i >= 3 * LAG) & (i < CHUNKS + 3 * LAG))
        def _():
            n = i - 3 * LAG
            cols = span(n)
            wait_bytes(grid_in.at[n, xm], x_recv.at[n, 0])
            block = grid_in.at[n, xm, low]
            remote(block, block, r_send.at[n, 0], r_recv.at[n, 0], right).start()
            wait_bytes(grid_in.at[n, xp], x_recv.at[n, 1])
            block = grid_in.at[n, xp, high]
            remote(block, block, r_send.at[n, 1], r_recv.at[n, 1], left).start()

        @pl.when(i >= 4 * LAG)
        def _():
            n = i - 4 * LAG
            cols = span(n)
            wait_bytes(grid_in.at[n, 0, 0], own_sem.at[n])
            wait_bytes(grid_in.at[n, xo, low], r_recv.at[n, 0])
            wait_bytes(grid_in.at[n, xo, high], r_recv.at[n, 1])
            weight = w1[span(n), :]
            for b in range(NX):
                hidden[b] += jnp.dot(
                    grid_in[n, b].reshape(NY * CAP, width),
                    weight,
                    preferred_element_type=jnp.float32,
                )

        return c

    lax.fori_loop(0, CHUNKS + 4 * LAG, inward, 0)
    for b in range(NX):
        v = hidden[b]
        act[b] = (v / (1.0 + jnp.exp(-v))).astype(jnp.bfloat16)
    load2.wait()

    def outward(i, c):
        @pl.when(i < CHUNKS)
        def _():
            cols = span(i)

            def product(b):
                part[i, b] = (
                    jnp.dot(act[b], w2[:, cols], preferred_element_type=jnp.float32)
                    .astype(jnp.bfloat16)
                    .reshape(NY, CAP, width)
                )

            product(xo)
            product(xm)
            product(xp)
            remote(
                part.at[i, xo, low], relay_in.at[i, 0],
                br_send.at[i, 0], br_recv.at[i, 0], left,
            ).start()
            remote(
                part.at[i, xo, high], relay_in.at[i, 1],
                br_send.at[i, 1], br_recv.at[i, 1], right,
            ).start()
            product(x)
            remote(
                part.at[i, xm, high], direct_in.at[i, 0, high],
                bd_send.at[i, 0], bd_recv.at[i, 0], left,
            ).start()
            remote(
                part.at[i, xp, low], direct_in.at[i, 1, low],
                bd_send.at[i, 1], bd_recv.at[i, 1], right,
            ).start()

        @pl.when((i >= 1 * LAG) & (i < CHUNKS + 1 * LAG))
        def _():
            n = i - 1 * LAG
            cols = span(n)

            def added(b, rows, side):
                wait_bytes(relay_in.at[n, side], br_recv.at[n, side])
                part[n, b, rows] = (
                    part[n, b, rows].astype(jnp.float32)
                    + relay_in[n, side].astype(jnp.float32)
                ).astype(jnp.bfloat16)

            added(xm, low, 0)
            added(xp, high, 1)
            remote(
                part.at[n, xm, low], direct_in.at[n, 0, low],
                bd_send.at[n, 2], bd_recv.at[n, 2], left,
            ).start()
            remote(
                part.at[n, xp, high], direct_in.at[n, 1, high],
                bd_send.at[n, 3], bd_recv.at[n, 3], right,
            ).start()

        @pl.when((i >= 2 * LAG) & (i < CHUNKS + 2 * LAG))
        def _():
            n = i - 2 * LAG
            cols = span(n)
            wait_bytes(direct_in.at[n, 0, high], bd_recv.at[n, 0])
            wait_bytes(direct_in.at[n, 1, low], bd_recv.at[n, 1])
            wait_bytes(direct_in.at[n, 0, low], bd_recv.at[n, 2])
            wait_bytes(direct_in.at[n, 1, high], bd_recv.at[n, 3])
            summed[n] = (
                part[n, x].astype(jnp.float32)
                + direct_in[n, 0].astype(jnp.float32)
                + direct_in[n, 1].astype(jnp.float32)
            ).astype(jnp.bfloat16)
            pltpu.make_async_copy(
                summed.at[n, 0], back.at[n, y], by_own.at[n]
            ).start()
            for j in range(1, NY):
                yd, dev = ydev(j)
                remote(
                    summed.at[n, j], back.at[n, y], by_send.at[n], by_recv.at[n], dev
                ).start()

        @pl.when((i >= 3 * LAG) & (i < CHUNKS + 3 * LAG))
        def _():
            n = i - 3 * LAG
            cols = span(n)
            wait_bytes(back.at[n, 0], by_own.at[n])
            wait_bytes(back.at[n, pl.ds(0, NY - 1)], by_recv.at[n])
            rows = back[n].reshape(NY * CAP, width)
            total = sum(
                lax.dot_general(
                    half[...].reshape(NY * CAP, NZ * 2 * TOK),
                    rows,
                    (((0,), (0,)), ((), ())),
                    preferred_element_type=jnp.float32,
                )
                for half in (mix_hi, mix_lo)
            )
            total = total.reshape(NZ, 2, -1, width)
            mixed[n] = total
            mixed_send[n] = total.astype(jnp.bfloat16)
            remote(
                mixed_send.at[n, :, other], core_in.at[n],
                bc_send.at[n], bc_recv.at[n], partner,
            ).start()

        @pl.when((i >= 4 * LAG) & (i < CHUNKS + 4 * LAG))
        def _():
            n = i - 4 * LAG
            cols = span(n)
            wait_bytes(core_in.at[n], bc_recv.at[n])
            z_out[n] = (
                mixed[n, :, core] + core_in[n].astype(jnp.float32)
            ).astype(jnp.bfloat16)
            pltpu.make_async_copy(z_out.at[n, z], z_in.at[n, z], bz_own.at[n]).start()
            for j in range(1, NZ):
                zd, dev = zdev(j)
                remote(
                    z_out.at[n, zd], z_in.at[n, z], bz_send.at[n], bz_recv.at[n], dev
                ).start()

        @pl.when(i >= 5 * LAG)
        def _():
            n = i - 5 * LAG
            cols = span(n)
            wait_bytes(z_in.at[n, 0], bz_own.at[n])
            wait_bytes(z_in.at[n, pl.ds(0, NZ - 1)], bz_recv.at[n])
            total = residual[:, cols]
            for k in range(NZ):
                total = total + z_in[n, k].astype(jnp.float32)
            out[:, cols] = total.astype(jnp.bfloat16)

        return c

    lax.fori_loop(0, CHUNKS + 5 * LAG, outward, 0)

    def drain(i, c):
        cols = span(i)
        half = relay_in.at[i, 0]
        wait_bytes(seven(i), y_send.at[i])
        for s in range(2):
            wait_bytes(grid_in.at[i, 0], x_send.at[i, s])
            wait_bytes(half, r_send.at[i, s])
            wait_bytes(half, br_send.at[i, s])
        for s in range(4):
            wait_bytes(half, bd_send.at[i, s])
        wait_bytes(back.at[i, pl.ds(0, NY - 1)], by_send.at[i])
        wait_bytes(z_in.at[i, pl.ds(0, NZ - 1)], z_send.at[i])
        wait_bytes(z_in.at[i], c_send.at[i])
        wait_bytes(z_in.at[i], bc_send.at[i])
        wait_bytes(z_in.at[i, pl.ds(0, NZ - 1)], bz_send.at[i])
        return c

    for copy in pages:
        copy.wait_send()
    lax.fori_loop(0, CHUNKS, drain, 0)


def body(
    resid_in,
    queries,
    fresh_kv,
    kv_pool,
    block_table,
    lengths,
    mig_source,
    mig_target,
    expert_ids,
    gate_values,
    norm_gain,
    w_in,
    w_out,
):
    depth, units = w_in.shape[2:]
    rows = resid_in.shape[0]
    pool = kv_pool[0, 0]
    page, wide = pool.shape[1:]
    count = expert_ids.shape[0]
    width = depth // CHUNKS
    bf = jnp.bfloat16
    vmem = pl.BlockSpec(memory_space=pltpu.VMEM)
    smem = pl.BlockSpec(memory_space=pltpu.SMEM)
    anywhere = pl.BlockSpec(memory_space=pl.ANY)
    dma = pltpu.SemaphoreType.DMA
    return pl.pallas_call(
        layer_kernel,
        name="whole_layer",
        out_shape=jax.ShapeDtypeStruct((rows, depth), bf),
        in_specs=[smem] * 4 + [vmem] * 7 + [anywhere] * 2,
        out_specs=vmem,
        scratch_shapes=[
            pltpu.VMEM((2, MIGP, page, wide), bf),
            pltpu.VMEM((2, MIGP, page, wide), bf),
            pltpu.VMEM((block_table.size * page, wide), bf),
            pltpu.VMEM((rows, depth), jnp.float32),
            pltpu.VMEM((rows, depth), bf),
            pltpu.VMEM((EXP_DEV, CAP, count), bf),
            pltpu.VMEM((NY, CAP, count), bf),
            pltpu.VMEM((NY, CAP, count), bf),
            pltpu.VMEM((CHUNKS, NZ, 2, rows, width), bf),
            pltpu.VMEM((CHUNKS, EXP_DEV, CAP, width), bf),
            pltpu.VMEM((CHUNKS, NZ, 2, rows, width), jnp.float32),
            pltpu.VMEM((CHUNKS, NZ, 2, rows, width), bf),
            pltpu.VMEM((CHUNKS, NZ, rows, width), bf),
            pltpu.VMEM((CHUNKS, NZ, rows, width), bf),
            pltpu.VMEM((CHUNKS, NZ, rows, width), bf),
            pltpu.VMEM((CHUNKS, NX, NY, CAP, width), bf),
            pltpu.VMEM((CHUNKS, NX, NY, CAP, width), bf),
            pltpu.VMEM((CHUNKS, 2, NY // 2, CAP, width), bf),
            pltpu.VMEM((CHUNKS, 2, NY, CAP, width), bf),
            pltpu.VMEM((CHUNKS, NY, CAP, width), bf),
            pltpu.VMEM((CHUNKS, NY, CAP, width), bf),
            pltpu.VMEM((depth, units), bf),
            pltpu.VMEM((units, depth), bf),
            pltpu.VMEM((NX, NY * CAP, units), jnp.float32),
            pltpu.VMEM((NX, NY * CAP, units), bf),
            dma((2,)),
            dma((2,)),
            dma((2,)),
            dma((CHUNKS,)),
            dma((CHUNKS,)),
            dma((CHUNKS,)),
            dma((CHUNKS, 2)),
            dma((CHUNKS, 2)),
            dma((CHUNKS, 2)),
            dma((CHUNKS, 2)),
            dma((CHUNKS, 2)),
            dma((CHUNKS, 2)),
            dma((CHUNKS, 4)),
            dma((CHUNKS, 4)),
            dma((CHUNKS,)),
            dma((CHUNKS,)),
            dma((CHUNKS,)),
        ]
        + [dma((CHUNKS,))] * 10,
        compiler_params=pltpu.CompilerParams(
            collective_id=0, has_side_effects=True, vmem_limit_bytes=56 * 1024 * 1024
        ),
    )(
        block_table,
        lengths,
        mig_source[0, 0],
        mig_target[0, 0],
        resid_in,
        queries,
        fresh_kv,
        pool,
        expert_ids.T,
        gate_values.T,
        norm_gain[None],
        w_in[0, 0],
        w_out[0, 0],
    )


def solution(mesh):
    placed = (
        P(("req", "exp"), None),
        P(("req", "exp"), None),
        P(("req", "exp"), None),
        P("req", "exp", None, None, None),
        P(("req", "exp"), None),
        P(("req", "exp")),
        P("req", "exp", None, None),
        P("req", "exp", None, None),
        P("req", None),
        P("req", None),
        P(),
        P("exp", "req", None, None),
        P("exp", "req", None, None),
    )
    return jax.shard_map(
        body, mesh=mesh, in_specs=placed, out_specs=P(("req", "exp"), None), check_vma=False
    )
```

```python
import functools

import jax
import jax.numpy as jnp
from jax import lax
from jax.experimental import pallas as pl
from jax.experimental.pallas import tpu as pltpu
from jax.sharding import PartitionSpec as P

HEADS = 28
KV_HEADS = 4
HEAD_DIM = 128
EXP_DEV = 4
CAP = 24
TOK = 8
MIGP = 4
NX = 4
NY = 8
NZ = 8
CHUNKS = 14
SHARED = 9
INWARD = (0, 1, 3, 5, 9, 7)
OUTWARD = (0, 4, 6, 8, 9, 11, 2)

neg_big = -1e30
norm_eps = 1e-06
MESH = pl.DeviceIdType.MESH


def wait_bytes(ref, sem):
    pltpu.make_async_copy(ref, ref, sem).wait()


def choose_slots(ex, ids, gates, select, mix_hi, mix_lo):
    count = ids.shape[1]
    earlier = lax.broadcasted_iota(jnp.int32, (count, count), 0)
    later = lax.broadcasted_iota(jnp.int32, (count, count), 1)
    upto = jnp.where(earlier <= later, 1.0, 0.0).astype(jnp.bfloat16)
    slot = lax.broadcasted_iota(jnp.int32, (CAP, count), 0).astype(jnp.float32) + 1.0
    for k in range(EXP_DEV):
        match = ids[...] == ex * EXP_DEV + k
        named = jnp.max(jnp.where(match, 1.0, 0.0), axis=0, keepdims=True)
        gate = jnp.sum(jnp.where(match, gates[...], 0.0), axis=0, keepdims=True)
        row = jnp.broadcast_to(named, (8, count)).astype(jnp.bfloat16)
        order = jnp.dot(row, upto, preferred_element_type=jnp.float32)[:1]
        placed = jnp.where(slot == order, 1.0, 0.0) * named
        select[k] = placed.astype(jnp.bfloat16)
        weight = placed * gate
        upper = weight.astype(jnp.bfloat16)
        lower = (weight - upper.astype(jnp.float32)).astype(jnp.bfloat16)
        for h in range(NY // EXP_DEV):
            mix_hi[k * (NY // EXP_DEV) + h] = upper
            mix_lo[k * (NY // EXP_DEV) + h] = lower


def stay_pages(table, pool, cache):
    requests, entries = table.shape
    page = pool.shape[1]
    rest = entries - MIGP

    def copy(i, c):
        n, p = lax.div(i, rest), MIGP + lax.rem(i, rest)
        start = pl.multiple_of((n * entries + p) * page, page)
        cache[pl.ds(start, page), :] = pool[table[n, p]]
        return c

    lax.fori_loop(0, requests * rest, copy, 0)


def attend(table, lengths, targets, resid_in, queries, fresh, pool, gain, arriving, cache, residual, normed):
    requests, entries = table.shape
    page = pool.shape[1]
    context = entries * page
    drafts = TOK // requests
    group = HEADS // KV_HEADS

    def gather(i, c):
        n, p = lax.div(i, MIGP), lax.rem(i, MIGP)
        entry = table[n, p]
        old = pool[entry].astype(jnp.float32)
        for side in range(2):
            moved = jnp.where(entry == targets[side, p], 1, 0)
            new = arriving[side, p].astype(jnp.float32)
            old = jnp.where(jnp.broadcast_to(moved, new.shape) > 0, new, old)
        start = pl.multiple_of((n * entries + p) * page, page)
        cache[pl.ds(start, page), :] = old.astype(jnp.bfloat16)
        return c

    lax.fori_loop(0, requests * MIGP, gather, 0)
    shape = (group * TOK, requests * context)
    token = lax.rem(lax.broadcasted_iota(jnp.int32, shape, 0), TOK)
    column = lax.broadcasted_iota(jnp.int32, shape, 1)
    holder = lax.div(column, context)
    limit = jnp.zeros(shape, jnp.int32)
    for n in range(requests):
        limit = jnp.where(holder == n, lengths[n], limit)
    cached = (lax.div(token, drafts) == holder) & (lax.rem(column, context) < limit)
    shape = (group * TOK, TOK)
    token = lax.rem(lax.broadcasted_iota(jnp.int32, shape, 0), TOK)
    column = lax.broadcasted_iota(jnp.int32, shape, 1)
    drafted = (lax.div(token, drafts) == lax.div(column, drafts)) & (column <= token)
    values = KV_HEADS * HEAD_DIM
    contract = (((1,), (1,)), ((), ()))

    def weighted(weights, rows):
        upper = weights.astype(jnp.bfloat16)
        lower = (weights - upper.astype(jnp.float32)).astype(jnp.bfloat16)
        return jnp.dot(upper, rows, preferred_element_type=jnp.float32) + jnp.dot(
            lower, rows, preferred_element_type=jnp.float32
        )

    squares = jnp.zeros((TOK, 1), jnp.float32)
    for kv in range(KV_HEADS):
        key_cols = slice(kv * HEAD_DIM, (kv + 1) * HEAD_DIM)
        value_cols = slice(values + kv * HEAD_DIM, values + (kv + 1) * HEAD_DIM)
        heads = [slice(h * HEAD_DIM, (h + 1) * HEAD_DIM) for h in range(kv * group, (kv + 1) * group)]
        query = jnp.concatenate([queries[:, h].astype(jnp.float32) for h in heads], axis=0).astype(
            jnp.bfloat16
        )
        far = lax.dot_general(
            query, cache[:, key_cols], contract, preferred_element_type=jnp.float32
        ) * HEAD_DIM ** (-0.5)
        near = lax.dot_general(
            query, fresh[:, key_cols], contract, preferred_element_type=jnp.float32
        ) * HEAD_DIM ** (-0.5)
        far = jnp.where(cached, far, neg_big)
        near = jnp.where(drafted, near, neg_big)
        highest = jnp.maximum(
            jnp.max(far, axis=1, keepdims=True), jnp.max(near, axis=1, keepdims=True)
        )
        far = jnp.where(cached, jnp.exp(far - highest), 0.0)
        near = jnp.where(drafted, jnp.exp(near - highest), 0.0)
        total = jnp.sum(far, axis=1, keepdims=True) + jnp.sum(near, axis=1, keepdims=True)
        attention = (
            weighted(far, cache[:, value_cols]) + weighted(near, fresh[:, value_cols])
        ) / total
        for g, h in enumerate(heads):
            mine = resid_in[:, h].astype(jnp.float32) + attention[g * TOK : (g + 1) * TOK]
            residual[:, h] = mine
            squares = squares + jnp.sum(mine * mine, axis=1, keepdims=True)
    inverse = lax.rsqrt(squares / (HEADS * HEAD_DIM) + norm_eps)
    normed[...] = (residual[...] * inverse * gain[...].astype(jnp.float32)).astype(jnp.bfloat16)


def layer_kernel(
    table,
    lengths,
    sources,
    targets,
    resid_in,
    queries,
    fresh,
    pool,
    ids,
    gates,
    gain,
    w_in,
    w_out,
    out,
    leaving,
    arriving,
    cache,
    residual,
    normed,
    select,
    mix_hi,
    mix_lo,
    tokens,
    packed,
    mixed,
    mixed_send,
    core_in,
    z_out,
    z_in,
    grid_in,
    part,
    relay_in,
    pair_in,
    direct_in,
    summed,
    back,
    w1,
    w2,
    hidden,
    act,
    load_sem,
    page_send,
    page_recv,
    own_sem,
    y_send,
    y_recv,
    x_send,
    x_recv,
    r_send,
    r_recv,
    br_send,
    br_recv,
    bd_send,
    bd_recv,
    by_own,
    by_send,
    by_recv,
    z_own,
    z_send,
    z_recv,
    c_send,
    c_recv,
    bc_send,
    bc_recv,
    bz_own,
    bz_send,
    bz_recv,
    p_send,
    p_recv,
    bp_send,
    bp_recv,
):
    me = lax.axis_index("req")
    ex = lax.axis_index("exp")
    x = lax.rem(me, NX)
    y = lax.div(me, NX)
    width = w1.shape[0] // CHUNKS
    row = y * NX
    xp = lax.rem(x + 1, NX)
    xm = lax.rem(x + NX - 1, NX)
    xo = lax.rem(x + 2, NX)
    ring = NX * NY
    after = (lax.rem(me + 1, ring), ex)
    before = (lax.rem(me + ring - 1, ring), ex)
    right = (row + xp, ex)
    left = (row + xm, ex)

    def ydev(j):
        yd = lax.rem(y + j, NY)
        return yd, (yd * NX + x, ex)

    z = lax.div(ex, 2)
    core = lax.rem(ex, 2)
    other = 1 - core
    partner = (me, z * 2 + other)

    def zdev(j):
        zd = lax.rem(z + j, NZ)
        return zd, (me, zd * 2 + core)

    barrier = pltpu.get_barrier_semaphore()
    for j in range(1, NZ):
        pl.semaphore_signal(barrier, inc=1, device_id=zdev(j)[1], device_id_type=MESH)
    for peer in (partner, left, right, after, before):
        pl.semaphore_signal(barrier, inc=1, device_id=peer, device_id_type=MESH)
    for j in range(1, NY):
        pl.semaphore_signal(barrier, inc=1, device_id=ydev(j)[1], device_id_type=MESH)
    load1 = pltpu.make_async_copy(w_in, w1, load_sem.at[0])
    load2 = pltpu.make_async_copy(w_out, w2, load_sem.at[1])
    load1.start()
    load2.start()
    for i in range(MIGP):
        leaving[0, i] = pool[sources[0, i]]
        leaving[1, i] = pool[sources[1, i]]
    hidden[...] = jnp.zeros_like(hidden)
    pl.semaphore_wait(barrier, 5 + NY - 1 + NZ - 1)

    def span(i):
        return pl.ds(pl.multiple_of(i * width, 128), width)

    def remote(src, dst, send, recv, dev):
        return pltpu.make_async_remote_copy(
            src_ref=src, dst_ref=dst, send_sem=send, recv_sem=recv, device_id=dev, device_id_type=MESH
        )

    pages = [
        remote(leaving.at[side], arriving.at[side], page_send.at[side], page_recv.at[side], dev)
        for side, dev in ((0, after), (1, before))
    ]
    for copy in pages:
        copy.start()
    choose_slots(ex, ids, gates, select, mix_hi, mix_lo)
    stay_pages(table, pool, cache)
    for copy in pages:
        copy.wait_recv()
    attend(table, lengths, targets, resid_in, queries, fresh, pool, gain, arriving, cache, residual, normed)

    def issue_z(i, c):
        cols = span(i)
        mine = tokens.at[i, z, core]
        pltpu.make_async_copy(normed.at[:, cols], mine, z_own.at[i]).start()
        for j in range(1, NZ):
            remote(normed.at[:, cols], mine, z_send.at[i], z_recv.at[i], zdev(j)[1]).start()
        return c

    lax.fori_loop(0, CHUNKS, issue_z, 0)
    load1.wait()
    low, high = pl.ds(0, NY // 2), pl.ds(NY // 2, NY // 2)
    odd = lax.rem(y, 2)
    twin = ((y + 1 - 2 * odd) * NX + x, ex)
    low_mine, high_mine = pl.ds(2 * odd, 2), pl.ds(NY // 2 + 2 * odd, 2)
    low_twin, high_twin = pl.ds(2 - 2 * odd, 2), pl.ds(NY // 2 + 2 - 2 * odd, 2)

    def seven(i):
        return grid_in.at[i, 0, pl.ds(0, NY - 1)]

    def inward(i, c):
        @pl.when(i < CHUNKS)
        def _():
            cols = span(i)
            wait_bytes(tokens.at[i, 0, 0], z_own.at[i])
            wait_bytes(tokens.at[i, pl.ds(0, NZ - 1), 0], z_recv.at[i])
            block = tokens.at[i, :, core]
            remote(block, block, c_send.at[i], c_recv.at[i], partner).start()

        @pl.when((i >= INWARD[1]) & (i < CHUNKS + INWARD[1]))
        def _():
            n = i - INWARD[1]
            cols = span(n)
            wait_bytes(tokens.at[n, :, 0], c_recv.at[n])
            packed[n] = (
                jnp.dot(
                    select[...].reshape(EXP_DEV * CAP, NZ * 2 * TOK),
                    tokens[n].reshape(NZ * 2 * TOK, width),
                    preferred_element_type=jnp.float32,
                )
                .astype(jnp.bfloat16)
                .reshape(EXP_DEV, CAP, width)
            )
            mine = packed.at[n, lax.div(y, 2)]
            spot = grid_in.at[n, x, y]
            pltpu.make_async_copy(mine, spot, own_sem.at[n]).start()
            remote(mine, spot, x_send.at[n, 0], x_recv.at[n, 0], right).start()
            remote(mine, spot, x_send.at[n, 1], x_recv.at[n, 1], left).start()
            for j in range(1, NY):
                yd, dev = ydev(j)
                remote(
                    packed.at[n, lax.div(yd, 2)],
                    spot,
                    y_send.at[n],
                    y_recv.at[n],
                    dev,
                ).start()

        @pl.when((i >= INWARD[2]) & (i < CHUNKS + INWARD[2]))
        def _():
            n = i - INWARD[2]
            cols = span(n)
            wait_bytes(seven(n), y_recv.at[n])
            for j in range(1, NY):
                block = grid_in.at[n, x, lax.rem(y + j, NY)]
                remote(block, block, x_send.at[n, 0], x_recv.at[n, 0], right).start()
                remote(block, block, x_send.at[n, 1], x_recv.at[n, 1], left).start()

        @pl.when((i >= INWARD[3]) & (i < CHUNKS + INWARD[3]))
        def _():
            n = i - INWARD[3]
            cols = span(n)
            wait_bytes(grid_in.at[n, xm], x_recv.at[n, 0])
            wait_bytes(grid_in.at[n, xp], x_recv.at[n, 1])

            def pass_on(first, second):
                block = grid_in.at[n, xm, first]
                remote(block, block, r_send.at[n, 0], r_recv.at[n, 0], right).start()
                block = grid_in.at[n, xp, second]
                remote(block, block, r_send.at[n, 1], r_recv.at[n, 1], left).start()

            @pl.when(n < SHARED)
            def _():
                pass_on(low_mine, high_mine)

            @pl.when(n >= SHARED)
            def _():
                pass_on(low, high)

        @pl.when((i >= INWARD[5]) & (i < SHARED + INWARD[5]))
        def _():
            n = i - INWARD[5]
            for side, rows in ((0, low_mine), (1, high_mine)):
                block = grid_in.at[n, xo, rows]
                wait_bytes(block, r_recv.at[n, side])
                remote(block, block, p_send.at[n], p_recv.at[n], twin).start()

        @pl.when(i >= INWARD[4])
        def _():
            n = i - INWARD[4]
            cols = span(n)
            wait_bytes(grid_in.at[n, 0, 0], own_sem.at[n])

            @pl.when(n < SHARED)
            def _():
                wait_bytes(grid_in.at[n, xo, low], p_recv.at[n])

            @pl.when(n >= SHARED)
            def _():
                wait_bytes(grid_in.at[n, xo, low], r_recv.at[n, 0])
                wait_bytes(grid_in.at[n, xo, high], r_recv.at[n, 1])

            weight = w1[span(n), :]
            for b in range(NX):
                hidden[b] += jnp.dot(
                    grid_in[n, b].reshape(NY * CAP, width),
                    weight,
                    preferred_element_type=jnp.float32,
                )

        return c

    lax.fori_loop(0, CHUNKS + INWARD[4], inward, 0)
    for b in range(NX):
        v = hidden[b]
        act[b] = (v / (1.0 + jnp.exp(-v))).astype(jnp.bfloat16)
    load2.wait()

    def outward(i, c):
        @pl.when(i < CHUNKS)
        def _():
            cols = span(i)

            def product(b):
                part[i, b] = (
                    jnp.dot(act[b], w2[:, cols], preferred_element_type=jnp.float32)
                    .astype(jnp.bfloat16)
                    .reshape(NY, CAP, width)
                )

            product(xo)

            @pl.when(i < SHARED)
            def _():
                for side, rows in ((0, low_twin), (1, high_twin)):
                    remote(
                        part.at[i, xo, rows], pair_in.at[i, side], bp_send.at[i], bp_recv.at[i], twin
                    ).start()

            @pl.when(i >= SHARED)
            def _():
                remote(
                    part.at[i, xo, low], relay_in.at[i, 0], br_send.at[i, 0], br_recv.at[i, 0], left
                ).start()
                remote(
                    part.at[i, xo, high], relay_in.at[i, 1], br_send.at[i, 1], br_recv.at[i, 1], right
                ).start()

            product(xm)
            product(xp)
            remote(
                part.at[i, xm, high], direct_in.at[i, 0, high],
                bd_send.at[i, 0], bd_recv.at[i, 0], left,
            ).start()
            remote(
                part.at[i, xp, low], direct_in.at[i, 1, low],
                bd_send.at[i, 1], bd_recv.at[i, 1], right,
            ).start()
            product(x)

        @pl.when((i >= OUTWARD[6]) & (i < SHARED + OUTWARD[6]))
        def _():
            n = i - OUTWARD[6]
            wait_bytes(pair_in.at[n], bp_recv.at[n])
            for side, rows, dev in ((0, low_mine, left), (1, high_mine, right)):
                part[n, xo, rows] = (
                    part[n, xo, rows].astype(jnp.float32) + pair_in[n, side].astype(jnp.float32)
                ).astype(jnp.bfloat16)
                remote(
                    part.at[n, xo, rows], relay_in.at[n, side, low_mine],
                    br_send.at[n, side], br_recv.at[n, side], dev,
                ).start()

        @pl.when((i >= OUTWARD[1]) & (i < CHUNKS + OUTWARD[1]))
        def _():
            n = i - OUTWARD[1]

            def added(b, rows, side, inner):
                wait_bytes(relay_in.at[n, side, inner], br_recv.at[n, side])
                part[n, b, rows] = (
                    part[n, b, rows].astype(jnp.float32)
                    + relay_in[n, side, inner].astype(jnp.float32)
                ).astype(jnp.bfloat16)

            @pl.when(n < SHARED)
            def _():
                added(xm, low_mine, 0, low_mine)
                added(xp, high_mine, 1, low_mine)

            @pl.when(n >= SHARED)
            def _():
                added(xm, low, 0, low)
                added(xp, high, 1, low)

            remote(
                part.at[n, xm, low], direct_in.at[n, 0, low],
                bd_send.at[n, 2], bd_recv.at[n, 2], left,
            ).start()
            remote(
                part.at[n, xp, high], direct_in.at[n, 1, high],
                bd_send.at[n, 3], bd_recv.at[n, 3], right,
            ).start()

        @pl.when((i >= OUTWARD[2]) & (i < CHUNKS + OUTWARD[2]))
        def _():
            n = i - OUTWARD[2]
            cols = span(n)
            wait_bytes(direct_in.at[n, 0, high], bd_recv.at[n, 0])
            wait_bytes(direct_in.at[n, 1, low], bd_recv.at[n, 1])
            wait_bytes(direct_in.at[n, 0, low], bd_recv.at[n, 2])
            wait_bytes(direct_in.at[n, 1, high], bd_recv.at[n, 3])
            summed[n] = (
                part[n, x].astype(jnp.float32)
                + direct_in[n, 0].astype(jnp.float32)
                + direct_in[n, 1].astype(jnp.float32)
            ).astype(jnp.bfloat16)
            pltpu.make_async_copy(
                summed.at[n, y], back.at[n, y], by_own.at[n]
            ).start()
            for j in range(1, NY):
                yd, dev = ydev(j)
                remote(
                    summed.at[n, yd], back.at[n, y], by_send.at[n], by_recv.at[n], dev
                ).start()

        @pl.when((i >= OUTWARD[3]) & (i < CHUNKS + OUTWARD[3]))
        def _():
            n = i - OUTWARD[3]
            cols = span(n)
            wait_bytes(back.at[n, 0], by_own.at[n])
            wait_bytes(back.at[n, pl.ds(0, NY - 1)], by_recv.at[n])
            rows = back[n].reshape(NY * CAP, width)
            total = sum(
                lax.dot_general(
                    half[...].reshape(NY * CAP, NZ * 2 * TOK),
                    rows,
                    (((0,), (0,)), ((), ())),
                    preferred_element_type=jnp.float32,
                )
                for half in (mix_hi, mix_lo)
            )
            total = total.reshape(NZ, 2, -1, width)
            mixed[n] = total
            mixed_send[n] = total.astype(jnp.bfloat16)
            remote(
                mixed_send.at[n, :, other], core_in.at[n],
                bc_send.at[n], bc_recv.at[n], partner,
            ).start()

        @pl.when((i >= OUTWARD[4]) & (i < CHUNKS + OUTWARD[4]))
        def _():
            n = i - OUTWARD[4]
            cols = span(n)
            wait_bytes(core_in.at[n], bc_recv.at[n])
            z_out[n] = (
                mixed[n, :, core] + core_in[n].astype(jnp.float32)
            ).astype(jnp.bfloat16)
            pltpu.make_async_copy(z_out.at[n, z], z_in.at[n, z], bz_own.at[n]).start()
            for j in range(1, NZ):
                zd, dev = zdev(j)
                remote(
                    z_out.at[n, zd], z_in.at[n, z], bz_send.at[n], bz_recv.at[n], dev
                ).start()

        @pl.when(i >= OUTWARD[5])
        def _():
            n = i - OUTWARD[5]
            cols = span(n)
            wait_bytes(z_in.at[n, 0], bz_own.at[n])
            wait_bytes(z_in.at[n, pl.ds(0, NZ - 1)], bz_recv.at[n])
            total = residual[:, cols]
            for k in range(NZ):
                total = total + z_in[n, k].astype(jnp.float32)
            out[:, cols] = total.astype(jnp.bfloat16)

        return c

    lax.fori_loop(0, CHUNKS + OUTWARD[5], outward, 0)

    def drain(i, c):
        cols = span(i)
        half = relay_in.at[i, 0]
        wait_bytes(seven(i), y_send.at[i])
        for s in range(2):
            wait_bytes(grid_in.at[i, 0], x_send.at[i, s])
        for s in range(4):
            wait_bytes(half, bd_send.at[i, s])
        wait_bytes(back.at[i, pl.ds(0, NY - 1)], by_send.at[i])

        @pl.when(i < SHARED)
        def _():
            for s in range(2):
                wait_bytes(pair_in.at[i, 0], r_send.at[i, s])
                wait_bytes(pair_in.at[i, 0], br_send.at[i, s])
            wait_bytes(pair_in.at[i], p_send.at[i])
            wait_bytes(pair_in.at[i], bp_send.at[i])

        @pl.when(i >= SHARED)
        def _():
            for s in range(2):
                wait_bytes(half, r_send.at[i, s])
                wait_bytes(half, br_send.at[i, s])

        wait_bytes(z_in.at[i, pl.ds(0, NZ - 1)], z_send.at[i])
        wait_bytes(z_in.at[i], c_send.at[i])
        wait_bytes(z_in.at[i], bc_send.at[i])
        wait_bytes(z_in.at[i, pl.ds(0, NZ - 1)], bz_send.at[i])
        return c

    for copy in pages:
        copy.wait_send()
    lax.fori_loop(0, CHUNKS, drain, 0)


def body(
    resid_in,
    queries,
    fresh_kv,
    kv_pool,
    block_table,
    lengths,
    mig_source,
    mig_target,
    expert_ids,
    gate_values,
    norm_gain,
    w_in,
    w_out,
):
    depth, units = w_in.shape[2:]
    rows = resid_in.shape[0]
    pool = kv_pool[0, 0]
    page, wide = pool.shape[1:]
    count = expert_ids.shape[0]
    width = depth // CHUNKS
    bf = jnp.bfloat16
    vmem = pl.BlockSpec(memory_space=pltpu.VMEM)
    smem = pl.BlockSpec(memory_space=pltpu.SMEM)
    anywhere = pl.BlockSpec(memory_space=pl.ANY)
    dma = pltpu.SemaphoreType.DMA
    return pl.pallas_call(
        layer_kernel,
        name="whole_layer",
        out_shape=jax.ShapeDtypeStruct((rows, depth), bf),
        in_specs=[smem] * 4 + [vmem] * 7 + [anywhere] * 2,
        out_specs=vmem,
        scratch_shapes=[
            pltpu.VMEM((2, MIGP, page, wide), bf),
            pltpu.VMEM((2, MIGP, page, wide), bf),
            pltpu.VMEM((block_table.size * page, wide), bf),
            pltpu.VMEM((rows, depth), jnp.float32),
            pltpu.VMEM((rows, depth), bf),
            pltpu.VMEM((EXP_DEV, CAP, count), bf),
            pltpu.VMEM((NY, CAP, count), bf),
            pltpu.VMEM((NY, CAP, count), bf),
            pltpu.VMEM((CHUNKS, NZ, 2, rows, width), bf),
            pltpu.VMEM((CHUNKS, EXP_DEV, CAP, width), bf),
            pltpu.VMEM((CHUNKS, NZ, 2, rows, width), jnp.float32),
            pltpu.VMEM((CHUNKS, NZ, 2, rows, width), bf),
            pltpu.VMEM((CHUNKS, NZ, rows, width), bf),
            pltpu.VMEM((CHUNKS, NZ, rows, width), bf),
            pltpu.VMEM((CHUNKS, NZ, rows, width), bf),
            pltpu.VMEM((CHUNKS, NX, NY, CAP, width), bf),
            pltpu.VMEM((CHUNKS, NX, NY, CAP, width), bf),
            pltpu.VMEM((CHUNKS, 2, NY // 2, CAP, width), bf),
            pltpu.VMEM((CHUNKS, 2, 2, CAP, width), bf),
            pltpu.VMEM((CHUNKS, 2, NY, CAP, width), bf),
            pltpu.VMEM((CHUNKS, NY, CAP, width), bf),
            pltpu.VMEM((CHUNKS, NY, CAP, width), bf),
            pltpu.VMEM((depth, units), bf),
            pltpu.VMEM((units, depth), bf),
            pltpu.VMEM((NX, NY * CAP, units), jnp.float32),
            pltpu.VMEM((NX, NY * CAP, units), bf),
            dma((2,)),
            dma((2,)),
            dma((2,)),
            dma((CHUNKS,)),
            dma((CHUNKS,)),
            dma((CHUNKS,)),
            dma((CHUNKS, 2)),
            dma((CHUNKS, 2)),
            dma((CHUNKS, 2)),
            dma((CHUNKS, 2)),
            dma((CHUNKS, 2)),
            dma((CHUNKS, 2)),
            dma((CHUNKS, 4)),
            dma((CHUNKS, 4)),
            dma((CHUNKS,)),
            dma((CHUNKS,)),
            dma((CHUNKS,)),
        ]
        + [dma((CHUNKS,))] * 14,
        compiler_params=pltpu.CompilerParams(
            collective_id=0, has_side_effects=True, vmem_limit_bytes=56 * 1024 * 1024
        ),
    )(
        block_table,
        lengths,
        mig_source[0, 0],
        mig_target[0, 0],
        resid_in,
        queries,
        fresh_kv,
        pool,
        expert_ids.T,
        gate_values.T,
        norm_gain[None],
        w_in[0, 0],
        w_out[0, 0],
    )


def solution(mesh):
    placed = (
        P(("req", "exp"), None),
        P(("req", "exp"), None),
        P(("req", "exp"), None),
        P("req", "exp", None, None, None),
        P(("req", "exp"), None),
        P(("req", "exp")),
        P("req", "exp", None, None),
        P("req", "exp", None, None),
        P("req", None),
        P("req", None),
        P(),
        P("exp", "req", None, None),
        P("exp", "req", None, None),
    )
    return jax.shard_map(
        body, mesh=mesh, in_specs=placed, out_specs=P(("req", "exp"), None), check_vma=False
    )
```
